256 devices in a mesh: chan: 16 (over z_hi, y, core), tm: 16 (over z_lo, x).
Axes of the slice: x: 4, y: 4, z: 8 (z_hi: 2, z_lo: 4; z = z_hi * 4 + z_lo), core: 2. Of those that a mesh axis runs over, the one named last changes fastest.
Arguments:
- signal: bfloat16 [256, 64, 8192], P('chan', None, 'tm'), may hold values from -6 to 6
- depth_weight: float32 [64, 7], replicated, may hold values from -2 to 2
- point_weight: bfloat16 [64, 64], replicated, may hold values from -0.75 to 0.75
- conv_weight: bfloat16 [3, 3, 64, 64], replicated, may hold values from -0.25 to 0.25
- grad_out: bfloat16 [128, 64, 4096], P('chan', None, 'tm'), may hold values from -6 to 6
Outputs:
- features_out: bfloat16 [128, 64, 4096], P('chan', None, 'tm')
- grad_signal: bfloat16 [256, 64, 8192], P('chan', None, 'tm')
- grad_depth: float32 [64, 7], replicated
- grad_point: float32 [64, 64], replicated
- grad_conv: float32 [3, 3, 64, 64], replicated
The draws below stay inside these ranges and needn't reach their ends.
All inputs are finite; a program needn't handle non-finite values.
Results may differ from the reference program's by a relative error of at most 0.0065.
Values may be sent and summed in bfloat16 or wider, within the bound.
A program may use at most 64 MiB of HBM per device.

```python
import jax
import jax.numpy as jnp
from jax import lax

F = 64
KERNEL_TAPS = 7
DILATION_STEP = 8
RIM = 24
CH_DEV = 16
NC = 256
TIME_SAMPLES = 8192
N_CHAN = 16


def levels(stream_key, shape, pieces, smallest, top_value):
    def one(axis_at, blocks):
        heights = jax.random.uniform(jax.random.fold_in(jax.random.fold_in(stream_key, 6), axis_at), (blocks,), jnp.float32, smallest / len(pieces), top_value / len(pieces))
        return jnp.repeat(jnp.exp(heights), shape[axis_at] // blocks).reshape((-1,) + (1,) * (len(shape) - axis_at - 1))

    factor_of = one(*pieces[0])
    for cut in pieces[1:]:
        factor_of = factor_of * one(*cut)
    return factor_of


def gaussian(own_key, dims, width, limit, pieces=(), kind=jnp.bfloat16):
    result = jax.random.normal(own_key, dims, jnp.float32) * width
    if len(pieces) > 0:
        result = levels(own_key, dims, pieces, -0.22, 0.18) * result
    return jnp.clip(result, min=-limit, max=limit).astype(kind)


def setup_inputs(seed: int = 0) -> dict:
    arg_keys = jax.random.split(jax.random.key(seed), 6)
    signal = gaussian(arg_keys[0], (NC, F, TIME_SAMPLES), 1.0, 6.0, ((0, 16), (2, 16)))
    depth_weight = gaussian(arg_keys[1], (F, KERNEL_TAPS), KERNEL_TAPS ** -0.5, 2.0, (), jnp.float32)
    point_weight = gaussian(arg_keys[2], (F, F), F ** -0.5, 0.75)
    conv_weight = gaussian(arg_keys[3], (3, 3, F, F), (9 * F) ** -0.5, 0.25)
    grad_out = gaussian(arg_keys[4], (NC // 2, F, TIME_SAMPLES // 2), 1.0, 6.0, ((0, 16), (2, 16)))
    return {"signal": signal, "depth_weight": depth_weight, "point_weight": point_weight, "conv_weight": conv_weight, "grad_out": grad_out}


def depthwise(extended_signal, weight, window_length):
    summed = jnp.zeros(extended_signal.shape[:2] + (window_length,), jnp.float32)
    for kernel_tap_index in range(KERNEL_TAPS):
        tap_segment = extended_signal[:, :, kernel_tap_index * DILATION_STEP:kernel_tap_index * DILATION_STEP + window_length].astype(jnp.float32)
        summed = summed + weight[:, kernel_tap_index][None, :, None].astype(jnp.float32) * tap_segment
    return summed

def conv_down(padded, weight):
    half_rows = (padded.shape[0] - 1) // 2
    half_cols = (padded.shape[2] - 1) // 2
    summed = jnp.zeros((half_rows, weight.shape[3], half_cols), jnp.float32)
    for row_tap in range(3):
        for col_tap in range(3):
            tap_segment = padded[row_tap:row_tap + 2 * half_rows:2, :, col_tap:col_tap + 2 * half_cols:2]
            summed = summed + jnp.einsum('cft,fg->cgt', tap_segment.astype(jnp.float32), weight[row_tap, col_tap].astype(jnp.float32))
    return summed

def conv_up(grad_ext, weight, half_rows, half_cols):
    parity_taps = {0: [(1, 0)], 1: [(0, 1), (2, 0)]}
    blocks = []
    for row_parity in (0, 1):
        inner_list = []
        for col_parity in (0, 1):
            summed = jnp.zeros((half_rows, weight.shape[2], half_cols), jnp.float32)
            for row_tap, row_skip in parity_taps[row_parity]:
                for col_tap, col_skip in parity_taps[col_parity]:
                    tap_segment = grad_ext[row_skip:row_skip + half_rows, :, col_skip:col_skip + half_cols]
                    summed = summed + jnp.einsum('cgt,fg->cft', tap_segment.astype(jnp.float32), weight[row_tap, col_tap].astype(jnp.float32))
            inner_list.append(summed)
        blocks.append(jnp.stack(inner_list, axis=-1))
    stacked = jnp.stack(blocks, axis=1)
    return stacked.reshape(2 * half_rows, weight.shape[2], 2 * half_cols)

def conv_grad(padded, grad_block):
    half_rows = grad_block.shape[0]
    half_cols = grad_block.shape[2]
    rows_list = []
    for row_tap in range(3):
        cols_list = []
        for col_tap in range(3):
            tap_segment = padded[row_tap:row_tap + 2 * half_rows:2, :, col_tap:col_tap + 2 * half_cols:2]
            cols_list.append(jnp.einsum('cft,cgt->fg', tap_segment.astype(jnp.float32), grad_block.astype(jnp.float32)))
        rows_list.append(jnp.stack(cols_list, axis=0))
    return jnp.stack(rows_list, axis=0)

def gelu_back(pre_act, upstream):
    unused_value, pullback = jax.vjp(jax.nn.gelu, pre_act)
    return pullback(upstream)[0]

def reference(signal, depth_weight, point_weight, conv_weight, grad_out):
    sig_pad = jnp.pad(signal, ((1, 0), (0, 0), (RIM, RIM)))
    grad_pad = jnp.pad(grad_out, ((0, 1), (0, 0), (0, 1)))

    def group_step(running, index):
        row_start = index * CH_DEV
        sig_block = lax.dynamic_slice_in_dim(sig_pad, row_start, CH_DEV + 1, 0)
        depth_low = depthwise(sig_block, depth_weight, TIME_SAMPLES).astype(jnp.bfloat16)
        mixed_pre = jnp.einsum('cft,fg->cgt', depth_low.astype(jnp.float32), point_weight.astype(jnp.float32))
        hidden = (sig_block[:, :, RIM:RIM + TIME_SAMPLES].astype(jnp.float32) + jax.nn.gelu(mixed_pre)).astype(jnp.bfloat16)
        padded = jnp.pad(hidden, ((0, 0), (0, 0), (1, 0)))
        out_block = conv_down(padded, conv_weight).astype(jnp.bfloat16)
        grad_ext = lax.dynamic_slice_in_dim(grad_pad, row_start // 2, CH_DEV // 2 + 1, 0)
        grad_hidden = conv_up(grad_ext, conv_weight, CH_DEV // 2, TIME_SAMPLES // 2)
        conv_part = conv_grad(padded, grad_ext[:CH_DEV // 2, :, :TIME_SAMPLES // 2])
        grad_mixed = gelu_back(mixed_pre[1:], grad_hidden).astype(jnp.bfloat16)
        low_own = depth_low[1:].astype(jnp.float32)
        point_part = jnp.einsum('cft,cgt->fg', low_own, grad_mixed.astype(jnp.float32))
        grad_depth_out = jnp.einsum('cgt,fg->cft', grad_mixed.astype(jnp.float32), point_weight.astype(jnp.float32))
        owned_extension = sig_block[1:]
        depth_list = []
        for kernel_tap_index in range(KERNEL_TAPS):
            tap_segment = owned_extension[:, :, kernel_tap_index * DILATION_STEP:kernel_tap_index * DILATION_STEP + TIME_SAMPLES].astype(jnp.float32)
            depth_list.append(lax.optimization_barrier(jnp.sum(tap_segment * grad_depth_out, axis=(0, 2))))
        depth_part = jnp.stack(depth_list, axis=1)
        grad_depth_pad = jnp.pad(grad_depth_out, ((0, 0), (0, 0), (RIM, RIM)))
        grad_signal = grad_hidden
        for kernel_tap_index in range(KERNEL_TAPS):
            start_offset = (KERNEL_TAPS - 1 - kernel_tap_index) * DILATION_STEP
            grad_signal = grad_signal + depth_weight[:, kernel_tap_index][None, :, None].astype(jnp.float32) * grad_depth_pad[:, :, start_offset:start_offset + TIME_SAMPLES]
        updated = (running[0] + depth_part, running[1] + point_part, running[2] + conv_part)
        return (updated, (out_block, grad_signal.astype(jnp.bfloat16)))
    initial = (jnp.zeros((F, KERNEL_TAPS), jnp.float32), jnp.zeros((F, F), jnp.float32), jnp.zeros((3, 3, F, F), jnp.float32))
    running, stacked = lax.scan(group_step, initial, jnp.arange(N_CHAN, dtype=jnp.int32))
    out_blocks, grad_blocks = stacked
    features_out = out_blocks.reshape(NC // 2, F, TIME_SAMPLES // 2)
    grad_signal = grad_blocks.reshape(NC, F, TIME_SAMPLES)
    return (features_out, grad_signal, running[0], running[1], running[2])
```

```python
import functools
import math

import jax
import jax.numpy as jnp
from jax import lax
from jax.experimental import pallas as pl
from jax.experimental.pallas import tpu as pltpu
from jax.sharding import PartitionSpec as P

F32, BF16 = jnp.float32, jnp.bfloat16
MESH = pl.DeviceIdType.MESH
TAPS = 7
RIM = 24
EDGE = 48
EDGE_G = 16
PLANE_UNITS = 32
EXTRA_UNITS = 9


def dot(a, b):
    return lax.dot_general(a, b, (((1,), (0,)), ((), ())), preferred_element_type=F32)


def dot_nt(a, b):
    return lax.dot_general(a, b, (((1,), (1,)), ((), ())), preferred_element_type=F32)


def select_matrix(rows, cols, offset=0):
    r = lax.broadcasted_iota(jnp.int32, (rows, cols), 0)
    c = lax.broadcasted_iota(jnp.int32, (rows, cols), 1)
    return jnp.where(c == r + offset, 1.0, 0.0).astype(BF16)


def loop(lo, hi, body):
    def step(i, carry):
        body(i)
        return carry

    lax.fori_loop(lo, hi, step, 0)


def halo_kernel(
    n_chan, n_tm, sig_l, sig_r, sig_row, go_l, go_r, go_row,
    out_l, out_r, out_row, out_go,
    send_l, send_r, got_l, got_r, got_row, got_go, corner_l, corner_r, ssem, rsem,
):
    a, b = lax.axis_index("chan"), lax.axis_index("tm")
    up, down = lax.rem(a + 1, n_chan), lax.rem(a + n_chan - 1, n_chan)
    right, left = lax.rem(b + 1, n_tm), lax.rem(b + n_tm - 1, n_tm)
    around = [(a, left), (a, right), (up, b), (down, b), (up, left), (up, right), (down, left), (down, right)]
    barrier = pltpu.get_barrier_semaphore()
    for device in around:
        pl.semaphore_signal(barrier, inc=1, device_id=device, device_id_type=MESH)

    pick_sl, pick_sr = select_matrix(EDGE, 128), select_matrix(EDGE, 128, 128 - EDGE)
    pick_gl, pick_gr = select_matrix(EDGE_G, 128), select_matrix(EDGE_G, 128, 128 - EDGE_G)
    zero = jnp.zeros((64, 128), BF16)
    for m in range(-1, 8):
        if m >= 0:
            send_l[m + 1, 0:EDGE] = dot_nt(pick_sl, sig_l[m]).astype(BF16)
            send_r[m + 1, 0:EDGE] = dot_nt(pick_sr, sig_r[m]).astype(BF16)
        for pick, src, dst in ((pick_gl, go_l, send_l), (pick_gr, go_r, send_r)):
            low = src[m] if m >= 0 else zero
            high = src[m + 1] if m < 7 else zero
            pair = jnp.concatenate([low, high], axis=0)
            dst[m + 1, EDGE:] = dot_nt(pick, pair).astype(BF16)
    pl.semaphore_wait(barrier, len(around))

    pieces = [
        (send_l.at[pl.ds(1, 8)], got_r.at[pl.ds(1, 8)]),
        (send_r.at[pl.ds(1, 8)], got_l.at[pl.ds(1, 8)]),
        (sig_row.at[0], got_row),
        (go_row.at[0], got_go),
        (send_l.at[8, pl.ds(0, EDGE)], got_r.at[0, pl.ds(0, EDGE)]),
        (send_r.at[8, pl.ds(0, EDGE)], got_l.at[0, pl.ds(0, EDGE)]),
        (send_l.at[0, pl.ds(EDGE, EDGE_G)], corner_r),
        (send_r.at[0, pl.ds(EDGE, EDGE_G)], corner_l),
    ]
    copies = []
    for n in (2, 3, 4, 5, 6, 7, 0, 1):
        src, dst = pieces[n]
        copies.append(
            pltpu.make_async_remote_copy(
                src_ref=src, dst_ref=dst, send_sem=ssem.at[n], recv_sem=rsem.at[n],
                device_id=around[n], device_id_type=MESH,
            )
        )
        copies[-1].start()
    for copy in copies:
        copy.wait()

    first_a, last_a = (a > 0).astype(F32), (a < n_chan - 1).astype(F32)
    first_b, last_b = (b > 0).astype(F32), (b < n_tm - 1).astype(F32)
    for got, out, corner, inside in ((got_l, out_l, corner_l, first_b), (got_r, out_r, corner_r, last_b)):
        out[0, 0:EDGE] = (got[0, 0:EDGE].astype(F32) * (inside * first_a)).astype(BF16)
        out[0, EDGE:] = jnp.zeros((EDGE_G, 128), BF16)
        for n in range(1, 8):
            out[n] = (got[n].astype(F32) * inside).astype(BF16)
        out[8, 0:EDGE] = (got[8, 0:EDGE].astype(F32) * inside).astype(BF16)
        tail = got[8, EDGE:].astype(F32) + corner[...].astype(F32) * last_a
        out[8, EDGE:] = (tail * inside).astype(BF16)
    out_row[...] = (got_row[...].astype(F32) * first_a).astype(BF16)
    out_go[...] = (got_go[...].astype(F32) * last_a).astype(BF16)


def halo_exchange(signal, grad_out, n_chan, n_tm):
    pairs = signal.reshape(8, 128, 512)
    vm = lambda shape, where: pl.BlockSpec(shape, lambda i, where=where: where)
    shapes = [(9, 64, 128), (9, 64, 128), (64, 512), (64, 256)]
    return pl.pallas_call(
        functools.partial(halo_kernel, n_chan, n_tm),
        grid=(1,),
        out_shape=[jax.ShapeDtypeStruct(s, BF16) for s in shapes],
        in_specs=[
            vm((8, 128, 128), (0, 0, 0)),
            vm((8, 128, 128), (0, 0, 3)),
            vm((1, 64, 512), (15, 0, 0)),
            vm((8, 64, 128), (0, 0, 0)),
            vm((8, 64, 128), (0, 0, 1)),
            vm((1, 64, 256), (0, 0, 0)),
        ],
        out_specs=[vm(s, (0,) * len(s)) for s in shapes],
        scratch_shapes=[pltpu.VMEM((9, 64, 128), BF16)] * 4
        + [pltpu.VMEM((64, 512), BF16), pltpu.VMEM((64, 256), BF16)]
        + [pltpu.VMEM((EDGE_G, 128), BF16)] * 2
        + [pltpu.SemaphoreType.DMA((8,))] * 2,
        compiler_params=pltpu.CompilerParams(collective_id=0, has_side_effects=True),
        name="halo",
    )(pairs, pairs, signal, grad_out, grad_out, grad_out)


def compute_kernel(
    n_tm, sig, go, halo_l, halo_r, row, go_next, dw, pw, cw,
    feat, gsig, part,
    xt, gp, ht, hp, go_ext, gt, gh_s, ga, gb, gd, acc_c, acc_m, eye, wup, cwt, pw2, pwt2, wrow,
):
    b = lax.axis_index("tm")

    eye[...] = select_matrix(256, 256)
    lane = lax.broadcasted_iota(jnp.int32, (64, 128), 1)
    sub = lax.broadcasted_iota(jnp.int32, (64, 128), 0)
    twice = jnp.where(lax.rem(lane, 64) == sub, 1.0, 0.0)
    twice16 = twice.astype(BF16)
    r128 = lax.broadcasted_iota(jnp.int32, (128, 128), 0)
    c128 = lax.broadcasted_iota(jnp.int32, (128, 128), 1)
    same = (r128 < 64) == (c128 < 64)
    wide = dot(pw[...], twice16).astype(BF16)
    wide = jnp.concatenate([wide, wide], axis=0).astype(F32)
    pw2[...] = jnp.where(same, wide, 0.0).astype(BF16)
    eye64 = select_matrix(64, 64)
    turned = dot_nt(eye64, pw[...]).astype(BF16)
    turned = dot(turned, twice16)
    turned = jnp.concatenate([turned, turned], axis=0)
    pwt2[...] = jnp.where(same, turned, 0.0).astype(BF16)
    zero64 = jnp.zeros((64, 64), BF16)
    wup[128:256, 0:128] = jnp.zeros((128, 128), BF16)
    for j in range(3):
        first = dot_nt(eye64, jnp.concatenate([zero64, cw[0, j]], axis=0)).astype(BF16)
        rest = dot_nt(eye64, jnp.concatenate([cw[1, j], cw[2, j]], axis=0)).astype(BF16)
        cwt[:, j * 256 : j * 256 + 128] = first
        cwt[:, j * 256 + 128 : j * 256 + 256] = rest
        at = {1: (0, 0), 2: (0, 128), 0: (128, 128)}[j]
        wup[at[0] : at[0] + 64, at[1] : at[1] + 128] = rest
        wup[at[0] + 64 : at[0] + 128, at[1] : at[1] + 128] = first
    for k in range(TAPS):
        wrow[k : k + 1, :] = jnp.sum(twice * dw[:, k : k + 1], axis=0, keepdims=True)

    c0 = math.sqrt(2.0 / math.pi)

    def forward(n, x):
        unit = eye[...]
        xt[n, 48:304] = dot_nt(unit, x[:, 0:256])
        xt[n, 304:560] = dot_nt(unit, x[:, 256:512])
        xt[n, 0:48] = halo_l[n, 0:EDGE].astype(F32)
        xt[n, 560:608] = halo_r[n, 0:EDGE].astype(F32)
        low = wrow[0:1, :] * xt[n, 0:560]
        for k in range(1, TAPS):
            low = low + wrow[k : k + 1, :] * xt[n, 8 * k : 8 * k + 560]
        pre = dot(low.astype(BF16), pw2[...])
        sq = pre * pre
        th = jnp.tanh(c0 * (pre + 0.044715 * (sq * pre)))
        cdf = 0.5 * (1.0 + th)
        hidden = (xt[n, 24:584] + pre * cdf).astype(BF16)
        ht[n] = hidden.astype(F32)
        gp[n] = cdf + (0.5 * pre) * (1.0 - th * th) * (c0 + (3 * 0.044715 * c0) * sq)

    forward(0, jnp.concatenate([jnp.zeros((64, 512), BF16), row[...]], axis=0))
    loop(0, 8, lambda m: forward(m + 1, sig[m]))

    @pl.when(b == 0)
    def _():
        for n in range(9):
            ht[n, 23:24] = jnp.zeros((1, 128), F32)
            gp[n, 0:24] = jnp.zeros((24, 128), F32)

    @pl.when(b == n_tm - 1)
    def _():
        for n in range(9):
            gp[n, 536:560] = jnp.zeros((24, 128), F32)

    def split(n):
        for j in range(3):
            hp[j, n] = ht[n, pl.ds(23 + j, 256, stride=2), :].astype(BF16)

    loop(0, 9, split)

    go_ext[0:512] = go[...].reshape(512, 256)
    go_ext[512:576] = go_next[...]
    acc_c[...] = jnp.zeros_like(acc_c)
    acc_m[...] = jnp.zeros_like(acc_m)

    def down(o):
        taps = jnp.concatenate([hp[j, o + s] for j in range(3) for s in range(2)], axis=1)
        acc_c[...] += dot(go[o], taps)
        feat[o] = dot_nt(cwt[...], taps).astype(BF16)

    loop(0, 8, down)

    def backward(m):
        unit = eye[...]
        x = go_ext[pl.ds(pl.multiple_of(m * 64, 64), 128), :]
        gt[0:16] = halo_l[m + 1, EDGE:].astype(F32)
        gt[16:272] = dot_nt(unit, x)
        gt[272:288] = halo_r[m + 1, EDGE:].astype(F32)
        gt[288:296] = jnp.zeros((8, 128), F32)
        both = jnp.concatenate([gt[0:288].astype(BF16), gt[1:289].astype(BF16)], axis=1)
        grads = dot(both, wup[...])
        gh_s[pl.ds(0, 288, stride=2), :] = grads[:, 0:128]
        gh_s[pl.ds(1, 288, stride=2), :] = grads[:, 128:256]
        mixed = gh_s[8:568] * gp[m + 1]
        mixed16 = mixed.astype(BF16)
        ga[...] = mixed16
        gb[0:552] = mixed[8:560].astype(BF16)
        shifted = []
        for k in range(TAPS):
            at = 48 - 8 * k
            shifted.append(ga[at : at + 512] if k % 2 == 0 else gb[at - 8 : at + 504])
        acc_m[...] += dot(sig[m], jnp.concatenate(shifted, axis=1))
        gd[...] = dot(mixed16, pwt2[...])
        total = gh_s[32:544]
        for k in range(TAPS):
            at = 48 - 8 * k
            total = total + wrow[k : k + 1, :] * gd[at : at + 512]
        gsig[m] = dot_nt(unit[0:128, 0:128], total.astype(BF16)).astype(BF16)

    loop(0, 8, backward)

    part[0:64] = acc_c[:, 128:256]
    part[64:128] = acc_c[:, 384:512]
    part[128:192] = acc_c[:, 640:768]
    part[192:256] = jnp.where(lane < 64, pltpu.roll(acc_c[:, 0:128], 64, 1), acc_c[:, 256:384])
    point = jnp.zeros((64, 128), F32)
    depth = jnp.zeros((64, 128), F32)
    pw_wide = jnp.where(lane < 64, dot(pw[...], twice16), 0.0)
    for k in range(TAPS):
        tap = acc_m[0:64, k * 128 : k * 128 + 128] + pltpu.roll(
            acc_m[64:128, k * 128 : k * 128 + 128], 64, 1
        )
        point = point + dw[:, k : k + 1] * tap
        depth = depth + jnp.where(lane == k, jnp.sum(tap * pw_wide, axis=1, keepdims=True), 0.0)
    part[256:320] = jnp.where(lane < 64, point, acc_c[:, 512:640])
    square = jnp.concatenate([depth, jnp.zeros((64, 128), F32)], axis=0)
    part[320:328] = jnp.transpose(square)[0:8]


def local_compute(signal, grad_out, halos, depth_weight, point_weight, conv_weight, n_tm):
    whole = pl.BlockSpec(memory_space=pltpu.VMEM)
    feat, gsig, part = pl.pallas_call(
        functools.partial(compute_kernel, n_tm),
        out_shape=[
            jax.ShapeDtypeStruct((8, 64, 256), BF16),
            jax.ShapeDtypeStruct((8, 128, 512), BF16),
            jax.ShapeDtypeStruct((328, 128), F32),
        ],
        in_specs=[whole] * 9,
        out_specs=[whole] * 3,
        scratch_shapes=[
            pltpu.VMEM((9, 608, 128), F32),
            pltpu.VMEM((9, 560, 128), F32),
            pltpu.VMEM((9, 560, 128), F32),
            pltpu.VMEM((3, 9, 256, 128), BF16),
            pltpu.VMEM((576, 256), BF16),
            pltpu.VMEM((296, 128), F32),
            pltpu.VMEM((576, 128), F32),
            pltpu.VMEM((560, 128), BF16),
            pltpu.VMEM((560, 128), BF16),
            pltpu.VMEM((560, 128), F32),
            pltpu.VMEM((64, 768), F32),
            pltpu.VMEM((128, 896), F32),
            pltpu.VMEM((256, 256), BF16),
            pltpu.VMEM((256, 256), BF16),
            pltpu.VMEM((64, 768), BF16),
            pltpu.VMEM((128, 128), BF16),
            pltpu.VMEM((128, 128), BF16),
            pltpu.VMEM((8, 128), F32),
        ],
        compiler_params=pltpu.CompilerParams(vmem_limit_bytes=48 * 1024 * 1024),
        name="compute",
    )(signal.reshape(8, 128, 512), grad_out, *halos, depth_weight, point_weight, conv_weight)
    return feat, gsig.reshape(16, 64, 512), part


def sum_kernel(
    low_chan, low_tm, n_chan, n_tm, part, depth_out, point_out, conv_out,
    plane_in, plane_x, mine, tower_in, done, ssem, rsem, xssem, xrsem,
):
    a, b = lax.axis_index("chan"), lax.axis_index("tm")
    plane = low_chan * low_tm
    tower = (n_chan // low_chan) * (n_tm // low_tm)
    a_hi, b_hi = lax.div(a, low_chan), lax.div(b, low_tm)
    a_lo, b_lo = lax.rem(a, low_chan), lax.rem(b, low_tm)
    me = a_lo * low_tm + b_lo
    level = a_hi * (n_tm // low_tm) + b_hi
    per = PLANE_UNITS // plane

    def in_plane(d):
        p = lax.rem(me + d, plane)
        return p, (a_hi * low_chan + lax.div(p, low_tm), b_hi * low_tm + lax.rem(p, low_tm))

    def in_tower(d):
        q = lax.rem(level + d, tower)
        hi = n_tm // low_tm
        return q, (lax.div(q, hi) * low_chan + a_lo, lax.rem(q, hi) * low_tm + b_lo)

    barrier = pltpu.get_barrier_semaphore()

    def greet(d):
        pl.semaphore_signal(barrier, inc=1, device_id=in_plane(d)[1], device_id_type=MESH)

    def greet_tower(d):
        pl.semaphore_signal(barrier, inc=1, device_id=in_tower(d)[1], device_id_type=MESH)

    loop(1, plane, greet)
    loop(1, tower, greet_tower)
    pl.semaphore_wait(barrier, plane + tower - 2)

    def to_owner(d):
        p, device = in_plane(d)
        return pltpu.make_async_remote_copy(
            src_ref=part.at[pl.ds(p * per, per)], dst_ref=plane_in.at[d],
            send_sem=ssem.at[0, d], recv_sem=rsem.at[0, d], device_id=device, device_id_type=MESH,
        )

    def to_owner_x(d):
        p, device = in_plane(d)
        return pltpu.make_async_remote_copy(
            src_ref=part.at[PLANE_UNITS + lax.rem(p, EXTRA_UNITS)], dst_ref=plane_x.at[d],
            send_sem=xssem.at[0, d], recv_sem=xrsem.at[0, d], device_id=device, device_id_type=MESH,
        )

    def send(d):
        to_owner(d).start()

        @pl.when(in_plane(d)[0] < EXTRA_UNITS)
        def _():
            to_owner_x(d).start()

    loop(1, plane, send)
    own_x = me < EXTRA_UNITS

    loop(1, plane, lambda d: to_owner(d).wait_recv())
    total = part[pl.ds(me * per, per)]
    for d in range(1, plane):
        total = total + plane_in[d]
    mine[0:per] = total

    def tower_copy(d, src, dst, s, r):
        return pltpu.make_async_remote_copy(
            src_ref=src, dst_ref=dst, send_sem=s, recv_sem=r,
            device_id=in_tower(d)[1], device_id_type=MESH,
        )

    def to_level(d):
        return tower_copy(d, mine.at[pl.ds(0, per)], tower_in.at[level, pl.ds(0, per)], ssem.at[1, d], rsem.at[1, d])

    def to_level_x(d):
        return tower_copy(d, mine.at[per], tower_in.at[level, per], xssem.at[1, d], xrsem.at[1, d])

    loop(1, tower, lambda d: to_level(d).start())

    @pl.when(own_x)
    def _():
        loop(1, plane, lambda d: to_owner_x(d).wait_recv())
        total = part[PLANE_UNITS + me]
        for d in range(1, plane):
            total = total + plane_x[d]
        mine[per] = total
        loop(1, tower, lambda d: to_level_x(d).start())

    tower_in[level, 0:per] = mine[0:per]
    loop(1, tower, lambda d: to_level(d).wait_recv())
    total = tower_in[0, 0:per]
    for q in range(1, tower):
        total = total + tower_in[q, 0:per]
    done[pl.ds(me * per, per)] = total

    def spread(d):
        return pltpu.make_async_remote_copy(
            src_ref=done.at[pl.ds(me * per, per)], dst_ref=done.at[pl.ds(me * per, per)],
            send_sem=ssem.at[2, d], recv_sem=rsem.at[2, d],
            device_id=in_plane(d)[1], device_id_type=MESH,
        )

    def spread_x(d):
        at = PLANE_UNITS + lax.rem(me, EXTRA_UNITS)
        return pltpu.make_async_remote_copy(
            src_ref=done.at[at], dst_ref=done.at[at],
            send_sem=xssem.at[2, d], recv_sem=xrsem.at[2, d],
            device_id=in_plane(d)[1], device_id_type=MESH,
        )

    loop(1, plane, lambda d: spread(d).start())

    @pl.when(own_x)
    def _():
        tower_in[level, per] = mine[per]
        loop(1, tower, lambda d: to_level_x(d).wait_recv())
        total = tower_in[0, per]
        for q in range(1, tower):
            total = total + tower_in[q, per]
        done[PLANE_UNITS + me] = total
        loop(1, plane, lambda d: spread_x(d).start())

    loop(1, plane, lambda d: spread(d).wait_recv())

    def arrive_x(d):
        p = lax.rem(me + plane - d, plane)

        @pl.when(p < EXTRA_UNITS)
        def _():
            spread_x(d).wait_recv()

    loop(1, plane, arrive_x)

    def left_all(d):
        to_owner(d).wait_send()
        spread(d).wait_send()

        @pl.when(in_plane(d)[0] < EXTRA_UNITS)
        def _():
            to_owner_x(d).wait_send()

        @pl.when(own_x)
        def _():
            spread_x(d).wait_send()

    loop(1, plane, left_all)

    def left_tower(d):
        to_level(d).wait_send()

        @pl.when(own_x)
        def _():
            to_level_x(d).wait_send()

    loop(1, tower, left_tower)

    def tile(n):
        return done[n * 8 : n * 8 + 8].reshape(64, 128)

    zero = jnp.zeros((64, 128), F32)
    for n in range(5):
        turned = jnp.transpose(jnp.concatenate([tile(n), zero], axis=0))
        for half in range(2):
            if n < 3:
                at = (half + 1, n)
            elif n == 3:
                at = (0, half)
            elif half == 1:
                at = (0, 2)
            else:
                point_out[...] = tile(4)[:, 0:64]
                continue
            conv_out[at[0], at[1]] = turned[half * 64 : half * 64 + 64, 0:64]
    depth = jnp.concatenate([done[40], jnp.zeros((120, 128), F32)], axis=0)
    depth_out[...] = jnp.transpose(depth)[0:64, 0:TAPS]


def sum_all(part, n_chan, n_tm):
    low_chan, low_tm = (8, 4) if n_chan == 16 else (2, 2)
    plane = low_chan * low_tm
    tower = n_chan * n_tm // plane
    per = PLANE_UNITS // plane
    whole = pl.BlockSpec(memory_space=pltpu.VMEM)
    sems = pltpu.SemaphoreType.DMA((3, plane))
    return pl.pallas_call(
        functools.partial(sum_kernel, low_chan, low_tm, n_chan, n_tm),
        out_shape=[
            jax.ShapeDtypeStruct((64, TAPS), F32),
            jax.ShapeDtypeStruct((64, 64), F32),
            jax.ShapeDtypeStruct((3, 3, 64, 64), F32),
        ],
        in_specs=[whole],
        out_specs=[whole] * 3,
        scratch_shapes=[
            pltpu.VMEM((plane, per, 8, 128), F32),
            pltpu.VMEM((plane, 8, 128), F32),
            pltpu.VMEM((per + 1, 8, 128), F32),
            pltpu.VMEM((tower, per + 1, 8, 128), F32),
            pltpu.VMEM((PLANE_UNITS + EXTRA_UNITS, 8, 128), F32),
            sems, sems, sems, sems,
        ],
        compiler_params=pltpu.CompilerParams(collective_id=1, has_side_effects=True),
        name="sum_all",
    )(part.reshape(PLANE_UNITS + EXTRA_UNITS, 8, 128))


def solution(mesh):
    n_chan, n_tm = mesh.shape["chan"], mesh.shape["tm"]

    def local(signal, depth_weight, point_weight, conv_weight, grad_out):
        halos = halo_exchange(signal, grad_out, n_chan, n_tm)
        feat, gsig, part = local_compute(
            signal, grad_out, halos, depth_weight, point_weight, conv_weight, n_tm
        )
        depth, point, conv = sum_all(part, n_chan, n_tm)
        return feat, gsig, depth, point, conv

    in_specs = (P("chan", None, "tm"), P(), P(), P(), P("chan", None, "tm"))
    out_specs = (P("chan", None, "tm"), P("chan", None, "tm"), P(), P(), P())
    return jax.shard_map(local, mesh=mesh, in_specs=in_specs, out_specs=out_specs, check_vma=False)
```

```python
import functools
import math

import jax
import jax.numpy as jnp
from jax import lax
from jax.experimental import pallas as pl
from jax.experimental.pallas import tpu as pltpu
from jax.sharding import PartitionSpec as P

F32, BF16 = jnp.float32, jnp.bfloat16
MESH = pl.DeviceIdType.MESH
TAPS = 7
RIM = 24
EDGE = 48
EDGE_G = 16
PLANE_UNITS = 32
EXTRA_UNITS = 9


def dot(a, b):
    return lax.dot_general(a, b, (((1,), (0,)), ((), ())), preferred_element_type=F32)


def dot_nt(a, b):
    return lax.dot_general(a, b, (((1,), (1,)), ((), ())), preferred_element_type=F32)


def select_matrix(rows, cols, offset=0):
    r = lax.broadcasted_iota(jnp.int32, (rows, cols), 0)
    c = lax.broadcasted_iota(jnp.int32, (rows, cols), 1)
    return jnp.where(c == r + offset, 1.0, 0.0).astype(BF16)


def loop(lo, hi, body):
    def step(i, carry):
        body(i)
        return carry

    lax.fori_loop(lo, hi, step, 0)


C0 = math.sqrt(2.0 / math.pi)
C1 = 0.044715 * C0


def gelu_parts(pre):
    sq = pre * pre
    th = jnp.tanh(pre * (C0 + C1 * sq))
    cdf = 0.5 + 0.5 * th
    value = pre * cdf
    slope = cdf + value * (1.0 - cdf) * (2.0 * C0 + (6.0 * C1) * sq)
    return value, slope


def kernel(
    low_chan, low_tm, n_chan, n_tm,
    sig, go, dw, pw, cw,
    feat, gsig, depth_out, point_out, conv_out,
    send_l, send_r, halo_l, halo_r, row, corner_l, corner_r,
    xt, gp, ht, hp, go_ext, gt, gh_s, ga, gb, gd, acc_m, eye, wup, cwt, pw2, pwt2, wrow,
    part, plane_in, plane_x, mine, tower_in, done,
    hssem, hrsem, ssem, rsem, xssem, xrsem,
):
    a, b = lax.axis_index("chan"), lax.axis_index("tm")
    plane = low_chan * low_tm
    hi_tm = n_tm // low_tm
    tower = (n_chan // low_chan) * hi_tm
    per = PLANE_UNITS // plane
    a_hi, b_hi = lax.div(a, low_chan), lax.div(b, low_tm)
    a_lo, b_lo = lax.rem(a, low_chan), lax.rem(b, low_tm)
    me = a_lo * low_tm + b_lo
    level = a_hi * hi_tm + b_hi
    before_a, after_a = a > 0, a < n_chan - 1
    before_b, after_b = b > 0, b < n_tm - 1
    both_of = jnp.logical_and

    def in_plane(d):
        p = lax.rem(me + d, plane)
        return p, (a_hi * low_chan + lax.div(p, low_tm), b_hi * low_tm + lax.rem(p, low_tm))

    def in_tower(d):
        q = lax.rem(level + d, tower)
        return q, (lax.div(q, hi_tm) * low_chan + a_lo, lax.rem(q, hi_tm) * low_tm + b_lo)

    def owns_extra(p):
        return both_of(lax.rem(p, 3) == 0, p < 3 * EXTRA_UNITS)

    around = [
        ((a, b - 1), before_b, after_b),
        ((a, b + 1), after_b, before_b),
        ((a + 1, b), after_a, before_a),
        ((a - 1, b), before_a, after_a),
        ((a + 1, b - 1), both_of(after_a, before_b), both_of(before_a, after_b)),
        ((a + 1, b + 1), both_of(after_a, after_b), both_of(before_a, before_b)),
        ((a - 1, b - 1), both_of(before_a, before_b), both_of(after_a, after_b)),
        ((a - 1, b + 1), both_of(before_a, after_b), both_of(after_a, before_b)),
    ]
    barrier = pltpu.get_barrier_semaphore()
    greeted = plane + tower - 2
    for device, there, _ in around:
        greeted = greeted + there.astype(jnp.int32)

        @pl.when(there)
        def _(device=device):
            pl.semaphore_signal(barrier, inc=1, device_id=device, device_id_type=MESH)

    def greet(d):
        pl.semaphore_signal(barrier, inc=1, device_id=in_plane(d)[1], device_id_type=MESH)

    def greet_tower(d):
        pl.semaphore_signal(barrier, inc=1, device_id=in_tower(d)[1], device_id_type=MESH)

    loop(1, tower, greet_tower)
    loop(1, plane, greet)

    pick_s, pick_g = select_matrix(EDGE, 128), select_matrix(EDGE_G, 128)
    pick_sr, pick_gr = select_matrix(EDGE, 128, 128 - EDGE), select_matrix(EDGE_G, 128, 128 - EDGE_G)
    zero16 = jnp.zeros((64, 128), BF16)
    for m in range(-1, 8):
        for pick, pick2, lanes, glanes, dst in (
            (pick_s, pick_g, slice(0, 128), slice(0, 128), send_l),
            (pick_sr, pick_gr, slice(384, 512), slice(128, 256), send_r),
        ):
            if m >= 0:
                dst[m + 1, 0:EDGE] = dot_nt(pick, sig[m, :, lanes]).astype(BF16)
            low = go[m, :, glanes] if m >= 0 else zero16
            high = go[m + 1, :, glanes] if m < 7 else zero16
            dst[m + 1, EDGE:] = dot_nt(pick2, jnp.concatenate([low, high], axis=0)).astype(BF16)

    eye[...] = select_matrix(256, 256)
    lane = lax.broadcasted_iota(jnp.int32, (64, 128), 1)
    sub = lax.broadcasted_iota(jnp.int32, (64, 128), 0)
    twice16 = jnp.where(lax.rem(lane, 64) == sub, 1.0, 0.0).astype(BF16)
    r128 = lax.broadcasted_iota(jnp.int32, (128, 128), 0)
    c128 = lax.broadcasted_iota(jnp.int32, (128, 128), 1)
    same = (r128 < 64) == (c128 < 64)
    wide = dot(pw[...], twice16)
    pw2[...] = jnp.where(same, jnp.concatenate([wide, wide], axis=0), 0.0).astype(BF16)
    eye64 = select_matrix(64, 64)
    turned = dot(dot_nt(eye64, pw[...]).astype(BF16), twice16)
    pwt2[...] = jnp.where(same, jnp.concatenate([turned, turned], axis=0), 0.0).astype(BF16)
    zero64 = jnp.zeros((64, 64), BF16)
    wup[128:256, 0:128] = jnp.zeros((128, 128), BF16)
    for j in range(3):
        first = dot_nt(eye64, jnp.concatenate([zero64, cw[0, j]], axis=0)).astype(BF16)
        rest = dot_nt(eye64, jnp.concatenate([cw[1, j], cw[2, j]], axis=0)).astype(BF16)
        cwt[:, j * 256 : j * 256 + 128] = first
        cwt[:, j * 256 + 128 : j * 256 + 256] = rest
        at = {1: (0, 0), 2: (0, 128), 0: (128, 128)}[j]
        wup[at[0] : at[0] + 64, at[1] : at[1] + 128] = rest
        wup[at[0] + 64 : at[0] + 128, at[1] : at[1] + 128] = first
    wrow[0:TAPS, 0:64] = dw[...]
    wrow[0:TAPS, 64:128] = dw[...]
    wrow[TAPS:, :] = jnp.zeros((1, 128), F32)

    def turn(n, x):
        unit = eye[...]
        xt[n, 48:304] = dot_nt(unit, x[:, 0:256])
        xt[n, 304:560] = dot_nt(unit, x[:, 256:512])

    loop(0, 4, lambda i: [turn(2 * i + s + 1, sig[2 * i + s]) for s in range(2)] and None)
    go_ext[0:512] = go[...].reshape(512, 256)

    pl.semaphore_wait(barrier, greeted)
    pieces = [
        (send_l.at[pl.ds(1, 8)], halo_r.at[pl.ds(1, 8)]),
        (send_r.at[pl.ds(1, 8)], halo_l.at[pl.ds(1, 8)]),
        (sig.at[7, pl.ds(64, 64)], row),
        (go.at[0], go_ext.at[pl.ds(512, 64)]),
        (send_l.at[8, pl.ds(0, EDGE)], halo_r.at[0, pl.ds(0, EDGE)]),
        (send_r.at[8, pl.ds(0, EDGE)], halo_l.at[0, pl.ds(0, EDGE)]),
        (send_l.at[0, pl.ds(EDGE, EDGE_G)], corner_r),
        (send_r.at[0, pl.ds(EDGE, EDGE_G)], corner_l),
    ]
    copies = [
        pltpu.make_async_remote_copy(
            src_ref=src, dst_ref=dst, send_sem=hssem.at[n], recv_sem=hrsem.at[n],
            device_id=around[n][0], device_id_type=MESH,
        )
        for n, (src, dst) in enumerate(pieces)
    ]
    for n in (2, 3, 0, 1, 4, 5, 6, 7):

        @pl.when(around[n][1])
        def _(n=n):
            copies[n].start()

    def arrive(n):
        dst = pieces[n][1]

        @pl.when(around[n][2])
        def _():
            copies[n].wait_recv()

        @pl.when(jnp.logical_not(around[n][2]))
        def _():
            dst[...] = jnp.zeros(dst.shape, BF16)

    def taps(n, lo, count):
        low = wrow[0:1, :] * xt[n, lo : lo + count]
        for k in range(1, TAPS):
            low = low + wrow[k : k + 1, :] * xt[n, lo + 8 * k : lo + 8 * k + count]
        return low.astype(BF16)

    def forward(n, lo, count, with_slope=True):
        value, slope = gelu_parts(dot(taps(n, lo, count), pw2[...]))
        ht[n, lo : lo + count] = (xt[n, lo + 24 : lo + 24 + count] + value).astype(BF16).astype(F32)
        if with_slope:
            gp[n, lo : lo + count] = slope

    loop(1, 9, lambda n: forward(n, 48, 464))
    arrive(0)
    arrive(1)
    for lo, src, at in ((0, halo_l, 0), (512, halo_r, 560)):
        for n in range(1, 9):
            xt[n, at : at + EDGE] = src[n, 0:EDGE].astype(F32)
        pre = dot(jnp.concatenate([taps(n, lo, 48) for n in range(1, 9)], axis=0), pw2[...])
        value, slope = gelu_parts(pre)
        for n in range(1, 9):
            mine_rows = slice((n - 1) * 48, n * 48)
            x = xt[n, lo + 24 : lo + 72]
            ht[n, lo : lo + 48] = (x + value[mine_rows]).astype(BF16).astype(F32)
            gp[n, lo : lo + 48] = slope[mine_rows]
    arrive(2)
    arrive(4)
    arrive(5)
    xt[0, 0:EDGE] = halo_l[0, 0:EDGE].astype(F32)
    turn(0, jnp.concatenate([jnp.zeros((64, 512), BF16), row[...]], axis=0))
    xt[0, 560:608] = halo_r[0, 0:EDGE].astype(F32)
    forward(0, 16, 528, False)

    @pl.when(b == 0)
    def _():
        for n in range(9):
            ht[n, 23:24] = jnp.zeros((1, 128), F32)
            gp[n, 0:24] = jnp.zeros((24, 128), F32)

    @pl.when(b == n_tm - 1)
    def _():
        for n in range(9):
            gp[n, 536:560] = jnp.zeros((24, 128), F32)

    for n in range(9):
        for j in range(3):
            hp[j, n] = ht[n, pl.ds(23 + j, 256, stride=2), :].astype(BF16)

    grads = []
    for j in range(3):
        total = jnp.zeros((64, 256), F32)
        for o in range(8):
            total = total + dot(go[o], jnp.concatenate([hp[j, o], hp[j, o + 1]], axis=1))
        grads.append(total)
        put(part, 8 * j, total[:, 128:256])
    put(part, 24, jnp.where(lane < 64, pltpu.roll(grads[0][:, 0:128], 64, 1), grads[1][:, 0:128]))
    last = grads[2][:, 0:128]

    def remote(src, dst, s, r, device):
        return pltpu.make_async_remote_copy(
            src_ref=src, dst_ref=dst, send_sem=s, recv_sem=r, device_id=device, device_id_type=MESH
        )

    def to_owner(d):
        p, device = in_plane(d)
        return remote(part.at[pl.ds(p * per, per)], plane_in.at[d], ssem.at[0, d], rsem.at[0, d], device)

    def to_owner_x(d):
        p, device = in_plane(d)
        unit = PLANE_UNITS + lax.rem(lax.div(p, 3), EXTRA_UNITS)
        return remote(part.at[unit], plane_x.at[d], xssem.at[0, d], xrsem.at[0, d], device)

    def to_level(d):
        src, dst = mine.at[pl.ds(0, per)], tower_in.at[level, pl.ds(0, per)]
        return remote(src, dst, ssem.at[1, d], rsem.at[1, d], in_tower(d)[1])

    def to_level_x(d):
        return remote(mine.at[per], tower_in.at[level, per], xssem.at[1, d], xrsem.at[1, d], in_tower(d)[1])

    def spread(d):
        at = done.at[pl.ds(me * per, per)]
        return remote(at, at, ssem.at[2, d], rsem.at[2, d], in_plane(d)[1])

    own_x = owns_extra(me)
    unit_x = PLANE_UNITS + lax.rem(lax.div(me, 3), EXTRA_UNITS)

    def spread_x(d):
        at = done.at[unit_x]
        return remote(at, at, xssem.at[2, d], xrsem.at[2, d], in_plane(d)[1])

    loop(1, plane, lambda d: to_owner(d).start())

    arrive(3)
    arrive(6)
    arrive(7)
    for halo, corner in ((halo_l, corner_l), (halo_r, corner_r)):
        halo[8, EDGE:] = (halo[8, EDGE:].astype(F32) + corner[...].astype(F32)).astype(BF16)

    def backward(i):
        unit = eye[...]
        lhs, rhs = [], []
        for s in range(2):
            m = 2 * i + s
            x = go_ext[pl.ds(pl.multiple_of(m * 64, 64), 128), :]
            gt[s, 0:16] = halo_l[m + 1, EDGE:].astype(F32)
            gt[s, 16:272] = dot_nt(unit, x)
            gt[s, 272:288] = halo_r[m + 1, EDGE:].astype(F32)
            gt[s, 288:296] = jnp.zeros((8, 128), F32)
            both = jnp.concatenate([gt[s, 0:288].astype(BF16), gt[s, 1:289].astype(BF16)], axis=1)
            up = dot(both, wup[...])
            gh_s[m, pl.ds(0, 288, stride=2), :] = up[:, 0:128]
            gh_s[m, pl.ds(1, 288, stride=2), :] = up[:, 128:256]
            mixed = gh_s[m, 8:568] * gp[m + 1]
            ga[m] = mixed.astype(BF16)
            gb[s, 0:552] = mixed[8:560].astype(BF16)
            shifted = []
            for k in range(TAPS):
                at = 48 - 8 * k
                shifted.append(ga[m, at : at + 512] if k % 2 == 0 else gb[s, at - 8 : at + 504])
            lhs.append(sig[m])
            rhs.append(jnp.concatenate(shifted, axis=1))
        acc_m[...] += dot(jnp.concatenate(lhs, axis=1), jnp.concatenate(rhs, axis=0))

    acc_m[...] = jnp.zeros_like(acc_m)
    loop(0, 4, backward)

    point = jnp.zeros((64, 128), F32)
    depth = jnp.zeros((64, 128), F32)
    pw_wide = jnp.where(lane < 64, dot(pw[...], twice16), 0.0)
    dw_col = jnp.transpose(jnp.concatenate([wrow[...], jnp.zeros((120, 128), F32)], axis=0))
    for k in range(TAPS):
        tap = acc_m[0:64, k * 128 : k * 128 + 128] + pltpu.roll(
            acc_m[64:128, k * 128 : k * 128 + 128], 64, 1
        )
        point = point + dw_col[0:64, k : k + 1] * tap
        depth = depth + jnp.where(lane == k, jnp.sum(tap * pw_wide, axis=1, keepdims=True), 0.0)
    put(part, 32, jnp.where(lane < 64, point, last))
    square = jnp.concatenate([depth, jnp.zeros((64, 128), F32)], axis=0)
    part[40] = jnp.transpose(square)[0:8]

    def send_x(d):
        @pl.when(owns_extra(in_plane(d)[0]))
        def _():
            to_owner_x(d).start()

    loop(1, plane, send_x)

    for o in range(8):
        wide_taps = jnp.concatenate([hp[j, o + s] for j in range(3) for s in range(2)], axis=1)
        feat[o] = dot_nt(cwt[...], wide_taps).astype(BF16)

    loop(1, plane, lambda d: to_owner(d).wait_recv())
    total = part[pl.ds(me * per, per)]
    for d in range(1, plane):
        total = total + plane_in[d]
    mine[0:per] = total
    loop(1, tower, lambda d: to_level(d).start())

    def finish(i):
        unit = eye[0:128, 0:128]
        for s in range(2):
            m = 2 * i + s
            gd[s] = dot(ga[m], pwt2[...])
            total = gh_s[m, 32:544]
            for k in range(TAPS):
                at = 48 - 8 * k
                total = total + wrow[k : k + 1, :] * gd[s, at : at + 512]
            gsig[m] = dot_nt(unit, total.astype(BF16)).astype(BF16)

    loop(0, 2, finish)

    @pl.when(own_x)
    def _():
        loop(1, plane, lambda d: to_owner_x(d).wait_recv())
        total = part[unit_x]
        for d in range(1, plane):
            total = total + plane_x[d]
        mine[per] = total
        loop(1, tower, lambda d: to_level_x(d).start())

    tower_in[level, 0:per] = mine[0:per]
    loop(1, tower, lambda d: to_level(d).wait_recv())
    total = tower_in[0, 0:per]
    for q in range(1, tower):
        total = total + tower_in[q, 0:per]
    done[pl.ds(me * per, per)] = total
    loop(1, plane, lambda d: spread(d).start())

    loop(2, 4, finish)

    @pl.when(own_x)
    def _():
        tower_in[level, per] = mine[per]
        loop(1, tower, lambda d: to_level_x(d).wait_recv())
        total = tower_in[0, per]
        for q in range(1, tower):
            total = total + tower_in[q, per]
        done[unit_x] = total
        loop(1, plane, lambda d: spread_x(d).start())

    def tile(n):
        return done[n * 8 : n * 8 + 8].reshape(64, 128)

    def conv_tile(n):
        zero = jnp.zeros((64, 128), F32)
        return jnp.transpose(jnp.concatenate([tile(n), zero], axis=0))

    loop(1, plane, lambda d: spread(d).wait_recv())
    for n in range(4):
        turned = conv_tile(n)
        for half in range(2):
            i, j = (half + 1, n) if n < 3 else (0, half)
            conv_out[i, j] = turned[half * 64 : half * 64 + 64, 0:64]

    def arrive_x(d):
        @pl.when(owns_extra(lax.rem(me + plane - d, plane)))
        def _():
            spread_x(d).wait_recv()

    loop(1, plane, arrive_x)
    conv_out[0, 2] = conv_tile(4)[64:128, 0:64]
    point_out[...] = tile(4)[:, 0:64]
    depth_out[...] = done[40][0:TAPS, 0:64]

    for n in range(8):

        @pl.when(around[n][1])
        def _(n=n):
            copies[n].wait_send()

    def left_all(d):
        to_owner(d).wait_send()
        spread(d).wait_send()

        @pl.when(owns_extra(in_plane(d)[0]))
        def _():
            to_owner_x(d).wait_send()

        @pl.when(own_x)
        def _():
            spread_x(d).wait_send()

    loop(1, plane, left_all)

    def left_tower(d):
        to_level(d).wait_send()

        @pl.when(own_x)
        def _():
            to_level_x(d).wait_send()

    loop(1, tower, left_tower)


def put(ref, unit, tile):
    ref[unit : unit + 8] = tile.reshape(8, 8, 128)


def solution(mesh):
    n_chan, n_tm = mesh.shape["chan"], mesh.shape["tm"]
    low_chan, low_tm = 8, 4
    plane = low_chan * low_tm
    tower = n_chan * n_tm // plane
    per = PLANE_UNITS // plane
    whole = pl.BlockSpec(memory_space=pltpu.VMEM)
    sems = pltpu.SemaphoreType.DMA((3, plane))
    vm = pltpu.VMEM

    def local(signal, depth_weight, point_weight, conv_weight, grad_out):
        feat, gsig, depth, point, conv = pl.pallas_call(
            functools.partial(kernel, low_chan, low_tm, n_chan, n_tm),
            out_shape=[
                jax.ShapeDtypeStruct((8, 64, 256), BF16),
                jax.ShapeDtypeStruct((8, 128, 512), BF16),
                jax.ShapeDtypeStruct((TAPS, 64), F32),
                jax.ShapeDtypeStruct((64, 64), F32),
                jax.ShapeDtypeStruct((3, 3, 64, 64), F32),
            ],
            in_specs=[whole] * 5,
            out_specs=[whole] * 5,
            scratch_shapes=[
                vm((9, 64, 128), BF16),
                vm((9, 64, 128), BF16),
                vm((9, 64, 128), BF16),
                vm((9, 64, 128), BF16),
                vm((64, 512), BF16),
                vm((EDGE_G, 128), BF16),
                vm((EDGE_G, 128), BF16),
                vm((9, 608, 128), F32),
                vm((9, 560, 128), F32),
                vm((9, 560, 128), F32),
                vm((3, 9, 256, 128), BF16),
                vm((576, 256), BF16),
                vm((2, 296, 128), F32),
                vm((8, 576, 128), F32),
                vm((8, 560, 128), BF16),
                vm((2, 560, 128), BF16),
                vm((2, 560, 128), F32),
                vm((128, 896), F32),
                vm((256, 256), BF16),
                vm((256, 256), BF16),
                vm((64, 768), BF16),
                vm((128, 128), BF16),
                vm((128, 128), BF16),
                vm((8, 128), F32),
                vm((PLANE_UNITS + EXTRA_UNITS, 8, 128), F32),
                vm((plane, per, 8, 128), F32),
                vm((plane, 8, 128), F32),
                vm((per + 1, 8, 128), F32),
                vm((tower, per + 1, 8, 128), F32),
                vm((PLANE_UNITS + EXTRA_UNITS, 8, 128), F32),
                pltpu.SemaphoreType.DMA((8,)),
                pltpu.SemaphoreType.DMA((8,)),
                sems, sems, sems, sems,
            ],
            compiler_params=pltpu.CompilerParams(
                collective_id=0, has_side_effects=True, vmem_limit_bytes=48 * 1024 * 1024
            ),
            name="step",
        )(signal.reshape(8, 128, 512), grad_out, depth_weight.T, point_weight, conv_weight)
        return feat, gsig.reshape(16, 64, 512), depth.T, point, conv

    in_specs = (P("chan", None, "tm"), P(), P(), P(), P("chan", None, "tm"))
    out_specs = (P("chan", None, "tm"), P("chan", None, "tm"), P(), P(), P())
    return jax.shard_map(local, mesh=mesh, in_specs=in_specs, out_specs=out_specs, check_vma=False)
```

```python
import functools
import math

import jax
import jax.numpy as jnp
from jax import lax
from jax.experimental import pallas as pl
from jax.experimental.pallas import tpu as pltpu
from jax.sharding import PartitionSpec as P

F32, BF16 = jnp.float32, jnp.bfloat16
MESH = pl.DeviceIdType.MESH
TAPS = 7
RIM = 24
EDGE = 48
EDGE_G = 16
PLANE_UNITS = 32
EXTRA_UNITS = 9
FWD_UNROLL = 2
BWD_UNROLL = 4


def dot(a, b):
    return lax.dot_general(a, b, (((1,), (0,)), ((), ())), preferred_element_type=F32)


def dot_nt(a, b):
    return lax.dot_general(a, b, (((1,), (1,)), ((), ())), preferred_element_type=F32)


def select_matrix(rows, cols, offset=0):
    r = lax.broadcasted_iota(jnp.int32, (rows, cols), 0)
    c = lax.broadcasted_iota(jnp.int32, (rows, cols), 1)
    return jnp.where(c == r + offset, 1.0, 0.0).astype(BF16)


def loop(lo, hi, body):
    def step(i, carry):
        body(i)
        return carry

    lax.fori_loop(lo, hi, step, 0)


C0 = math.sqrt(2.0 / math.pi)
C1 = 0.044715 * C0


def gelu_cdf(pre):
    return 0.5 + 0.5 * jnp.tanh(pre * (C0 + C1 * (pre * pre)))


def gelu_slope(pre, cdf):
    return cdf + (pre * cdf) * (1.0 - cdf) * (2.0 * C0 + (6.0 * C1) * (pre * pre))


def kernel(
    low_chan, low_tm, n_chan, n_tm,
    sig_hbm, go_hbm, dw_hbm, pw_hbm, cw_hbm,
    feat, gsig, depth_out, point_out, conv_out,
    sig, go, dw, pw, cw, insem,
    send_l, send_r, halo_l, halo_r, row, corner_l, corner_r,
    xt, pre_s, cdf_s, ht, hp, go_ext, gt, gh_s, ga, gb, gd, acc_m, eye, wup, cwt, pw2, pwt2, wrow,
    part, plane_in, plane_x, mine, tower_in, tower_x, done,
    hssem, hrsem, ssem, rsem, xssem, xrsem,
):
    loads = [
        pltpu.make_async_copy(src, dst, insem.at[n])
        for n, (src, dst) in enumerate(
            ((sig_hbm, sig), (go_hbm, go), (dw_hbm, dw), (pw_hbm, pw), (cw_hbm, cw))
        )
    ]
    for load in loads:
        load.start()

    a, b = lax.axis_index("chan"), lax.axis_index("tm")
    plane = low_chan * low_tm
    hi_tm = n_tm // low_tm
    tower = (n_chan // low_chan) * hi_tm
    a_hi, b_hi = lax.div(a, low_chan), lax.div(b, low_tm)
    a_lo, b_lo = lax.rem(a, low_chan), lax.rem(b, low_tm)
    me = a_lo * low_tm + b_lo
    level = a_hi * hi_tm + b_hi
    before_a, after_a = a > 0, a < n_chan - 1
    before_b, after_b = b > 0, b < n_tm - 1
    both_of = jnp.logical_and

    rows_at = [lax.rem(a_lo + i, low_chan) for i in range(low_chan)]
    cols_at = [lax.rem(b_lo + j, low_tm) for j in range(low_tm)]
    in_plane = [
        (r * low_tm + c, (a_hi * low_chan + r, b_hi * low_tm + c))
        for i, r in enumerate(rows_at)
        for j, c in enumerate(cols_at)
        if i + j > 0
    ]
    hi_chan = n_chan // low_chan
    levels_a = [lax.rem(a_hi + i, hi_chan) * low_chan + a_lo for i in range(hi_chan)]
    levels_b = [lax.rem(b_hi + j, hi_tm) * low_tm + b_lo for j in range(hi_tm)]
    in_tower = [
        (ra, rb) for i, ra in enumerate(levels_a) for j, rb in enumerate(levels_b) if i + j > 0
    ]

    owners = [3 * u for u in range(EXTRA_UNITS)]
    own_x = both_of(lax.rem(me, 3) == 0, me < 3 * EXTRA_UNITS)
    unit_x = PLANE_UNITS + lax.rem(lax.div(me, 3), EXTRA_UNITS)

    around = [
        ((a, b - 1), before_b, after_b),
        ((a, b + 1), after_b, before_b),
        ((a + 1, b), after_a, before_a),
        ((a - 1, b), before_a, after_a),
        ((a + 1, b - 1), both_of(after_a, before_b), both_of(before_a, after_b)),
        ((a + 1, b + 1), both_of(after_a, after_b), both_of(before_a, before_b)),
        ((a - 1, b - 1), both_of(before_a, before_b), both_of(after_a, after_b)),
        ((a - 1, b + 1), both_of(before_a, after_b), both_of(after_a, before_b)),
    ]
    barrier = pltpu.get_barrier_semaphore()
    greeted = plane + tower - 2
    for device, there, _ in around:
        greeted = greeted + there.astype(jnp.int32)

        @pl.when(there)
        def _(device=device):
            pl.semaphore_signal(barrier, inc=1, device_id=device, device_id_type=MESH)

    for device in in_tower + [device for _, device in in_plane]:
        pl.semaphore_signal(barrier, inc=1, device_id=device, device_id_type=MESH)

    eye[...] = select_matrix(256, 256)
    for load in loads[2:]:
        load.wait()
    lane = lax.broadcasted_iota(jnp.int32, (64, 128), 1)
    sub = lax.broadcasted_iota(jnp.int32, (64, 128), 0)
    twice16 = jnp.where(lax.rem(lane, 64) == sub, 1.0, 0.0).astype(BF16)
    r128 = lax.broadcasted_iota(jnp.int32, (128, 128), 0)
    c128 = lax.broadcasted_iota(jnp.int32, (128, 128), 1)
    same = (r128 < 64) == (c128 < 64)
    wide = dot(pw[...], twice16)
    pw2[...] = jnp.where(same, jnp.concatenate([wide, wide], axis=0), 0.0).astype(BF16)
    eye64 = select_matrix(64, 64)
    turned = dot(dot_nt(eye64, pw[...]).astype(BF16), twice16)
    pwt2[...] = jnp.where(same, jnp.concatenate([turned, turned], axis=0), 0.0).astype(BF16)
    zero64 = jnp.zeros((64, 64), BF16)
    wup[128:256, 0:128] = jnp.zeros((128, 128), BF16)
    for j in range(3):
        first = dot_nt(eye64, jnp.concatenate([zero64, cw[0, j]], axis=0)).astype(BF16)
        rest = dot_nt(eye64, jnp.concatenate([cw[1, j], cw[2, j]], axis=0)).astype(BF16)
        cwt[:, j * 256 : j * 256 + 128] = first
        cwt[:, j * 256 + 128 : j * 256 + 256] = rest
        at = {1: (0, 0), 2: (0, 128), 0: (128, 128)}[j]
        wup[at[0] : at[0] + 64, at[1] : at[1] + 128] = rest
        wup[at[0] + 64 : at[0] + 128, at[1] : at[1] + 128] = first
    wrow[0:TAPS, 0:64] = dw[...]
    wrow[0:TAPS, 64:128] = dw[...]
    wrow[TAPS:, :] = jnp.zeros((1, 128), F32)

    loads[1].wait()
    loads[0].wait()

    pick_s, pick_g = select_matrix(EDGE, 128), select_matrix(EDGE_G, 128)
    pick_sr, pick_gr = select_matrix(EDGE, 128, 128 - EDGE), select_matrix(EDGE_G, 128, 128 - EDGE_G)
    zero16 = jnp.zeros((64, 128), BF16)
    for m in range(-1, 8):
        for pick, pick2, lanes, glanes, dst in (
            (pick_s, pick_g, slice(0, 128), slice(0, 128), send_l),
            (pick_sr, pick_gr, slice(384, 512), slice(128, 256), send_r),
        ):
            if m >= 0:
                dst[m + 1, 0:EDGE] = dot_nt(pick, sig[m, :, lanes]).astype(BF16)
            low = go[m, :, glanes] if m >= 0 else zero16
            high = go[m + 1, :, glanes] if m < 7 else zero16
            dst[m + 1, EDGE:] = dot_nt(pick2, jnp.concatenate([low, high], axis=0)).astype(BF16)

    pl.semaphore_wait(barrier, greeted)
    pieces = [
        (send_l.at[pl.ds(1, 8)], halo_r.at[pl.ds(1, 8)]),
        (send_r.at[pl.ds(1, 8)], halo_l.at[pl.ds(1, 8)]),
        (sig.at[7, pl.ds(64, 64)], row),
        (go.at[0], go_ext.at[pl.ds(512, 64)]),
        (send_l.at[8, pl.ds(0, EDGE)], halo_r.at[0, pl.ds(0, EDGE)]),
        (send_r.at[8, pl.ds(0, EDGE)], halo_l.at[0, pl.ds(0, EDGE)]),
        (send_l.at[0, pl.ds(EDGE, EDGE_G)], corner_r),
        (send_r.at[0, pl.ds(EDGE, EDGE_G)], corner_l),
    ]
    copies = [
        pltpu.make_async_remote_copy(
            src_ref=src, dst_ref=dst, send_sem=hssem.at[n], recv_sem=hrsem.at[n],
            device_id=around[n][0], device_id_type=MESH,
        )
        for n, (src, dst) in enumerate(pieces)
    ]
    for n in (2, 3, 0, 1, 4, 5, 6, 7):

        @pl.when(around[n][1])
        def _(n=n):
            copies[n].start()

    def arrive(n):
        dst = pieces[n][1]

        @pl.when(around[n][2])
        def _():
            copies[n].wait_recv()

        @pl.when(jnp.logical_not(around[n][2]))
        def _():
            dst[...] = jnp.zeros(dst.shape, BF16)

    def turn(n, x):
        unit = eye[...]
        xt[n, 48:304] = dot_nt(unit, x[:, 0:256])
        xt[n, 304:560] = dot_nt(unit, x[:, 256:512])

    for m in range(8):
        turn(m + 1, sig[m])
    go_ext[0:512] = go[...].reshape(512, 256)

    def taps(n, lo, count):
        low = wrow[0:1, :] * xt[n, lo : lo + count]
        for k in range(1, TAPS):
            low = low + wrow[k : k + 1, :] * xt[n, lo + 8 * k : lo + 8 * k + count]
        return low.astype(BF16)

    def forward(n, lo, count, keep=True):
        pre = dot(taps(n, lo, count), pw2[...])
        cdf = gelu_cdf(pre)
        ht[n, lo : lo + count] = xt[n, lo + 24 : lo + 24 + count] + pre * cdf
        if keep:
            pre_s[n, lo : lo + count] = pre
            cdf_s[n, lo : lo + count] = cdf

    def forward_some(i):
        for s in range(FWD_UNROLL):
            forward(FWD_UNROLL * i + 1 + s, 48, 464)

    loop(0, 8 // FWD_UNROLL, forward_some)
    arrive(0)
    arrive(1)
    for lo, src, at in ((0, halo_l, 0), (512, halo_r, 560)):
        for n in range(1, 9):
            xt[n, at : at + EDGE] = src[n, 0:EDGE].astype(F32)
        pre = dot(jnp.concatenate([taps(n, lo, 48) for n in range(1, 9)], axis=0), pw2[...])
        cdf = gelu_cdf(pre)
        value = pre * cdf
        for n in range(1, 9):
            own_rows = slice((n - 1) * 48, n * 48)
            ht[n, lo : lo + 48] = xt[n, lo + 24 : lo + 72] + value[own_rows]
            pre_s[n, lo : lo + 48] = pre[own_rows]
            cdf_s[n, lo : lo + 48] = cdf[own_rows]
    arrive(2)
    arrive(4)
    arrive(5)
    xt[0, 0:EDGE] = halo_l[0, 0:EDGE].astype(F32)
    turn(0, jnp.concatenate([jnp.zeros((64, 512), BF16), row[...]], axis=0))
    xt[0, 560:608] = halo_r[0, 0:EDGE].astype(F32)
    forward(0, 16, 528, False)

    @pl.when(b == 0)
    def _():
        for n in range(9):
            ht[n, 23:24] = jnp.zeros((1, 128), F32)
            pre_s[n, 0:24] = jnp.zeros((24, 128), F32)
            cdf_s[n, 0:24] = jnp.zeros((24, 128), F32)

    @pl.when(b == n_tm - 1)
    def _():
        for n in range(9):
            pre_s[n, 536:560] = jnp.zeros((24, 128), F32)
            cdf_s[n, 536:560] = jnp.zeros((24, 128), F32)

    for n in range(9):
        for j in range(3):
            hp[j, n] = ht[n, pl.ds(23 + j, 256, stride=2), :].astype(BF16)

    grads = []
    for j in range(3):
        total = jnp.zeros((64, 256), F32)
        for o in range(8):
            total = total + dot(go[o], jnp.concatenate([hp[j, o], hp[j, o + 1]], axis=1))
        grads.append(total)
        put(part, 8 * j, total[:, 128:256])
    put(part, 24, jnp.where(lane < 64, pltpu.roll(grads[0][:, 0:128], 64, 1), grads[1][:, 0:128]))
    last = grads[2][:, 0:128]

    def remote(src, dst, s, r, device):
        return pltpu.make_async_remote_copy(
            src_ref=src, dst_ref=dst, send_sem=s, recv_sem=r, device_id=device, device_id_type=MESH
        )

    def several(ref, count, sem_s, sem_r):
        at = ref.at[pl.ds(0, count)]
        return remote(at, at, sem_s, sem_r, in_plane[0][1])

    for p, device in in_plane:
        remote(part.at[p], plane_in.at[me], ssem.at[0], rsem.at[0], device).start()

    arrive(3)
    arrive(6)
    arrive(7)
    for halo, corner in ((halo_l, corner_l), (halo_r, corner_r)):
        halo[8, EDGE:] = (halo[8, EDGE:].astype(F32) + corner[...].astype(F32)).astype(BF16)

    def backward(i):
        unit = eye[...]
        lhs, rhs = [], []
        for s in range(BWD_UNROLL):
            m = BWD_UNROLL * i + s
            x = go_ext[pl.ds(pl.multiple_of(m * 64, 64), 128), :]
            gt[s, 0:16] = halo_l[m + 1, EDGE:].astype(F32)
            gt[s, 16:272] = dot_nt(unit, x)
            gt[s, 272:288] = halo_r[m + 1, EDGE:].astype(F32)
            gt[s, 288:296] = jnp.zeros((8, 128), F32)
            both = jnp.concatenate([gt[s, 0:288].astype(BF16), gt[s, 1:289].astype(BF16)], axis=1)
            up = dot(both, wup[...])
            gh_s[m, pl.ds(0, 288, stride=2), :] = up[:, 0:128]
            gh_s[m, pl.ds(1, 288, stride=2), :] = up[:, 128:256]
            mixed = gh_s[m, 8:568] * gelu_slope(pre_s[m + 1], cdf_s[m + 1])
            ga[m] = mixed.astype(BF16)
            gb[s, 0:552] = mixed[8:560].astype(BF16)
            shifted = []
            for k in range(TAPS):
                at = 48 - 8 * k
                shifted.append(ga[m, at : at + 512] if k % 2 == 0 else gb[s, at - 8 : at + 504])
            lhs.append(sig[m])
            rhs.append(jnp.concatenate(shifted, axis=1))
        acc_m[...] += dot(jnp.concatenate(lhs, axis=1), jnp.concatenate(rhs, axis=0))

    acc_m[...] = jnp.zeros_like(acc_m)
    dw_col = jnp.transpose(jnp.concatenate([wrow[...], jnp.zeros((120, 128), F32)], axis=0))
    loop(0, 8 // BWD_UNROLL, backward)

    point = jnp.zeros((64, 128), F32)
    pw_wide = jnp.where(lane < 64, dot(pw[...], twice16), 0.0)
    products = []
    for k in range(TAPS):
        tap = acc_m[0:64, k * 128 : k * 128 + 128] + pltpu.roll(
            acc_m[64:128, k * 128 : k * 128 + 128], 64, 1
        )
        point = point + dw_col[0:64, k : k + 1] * tap
        products.append(tap * pw_wide)
    put(part, 32, jnp.where(lane < 64, point, last))
    product = jnp.concatenate(products, axis=1)
    piece_h = product.astype(BF16)
    rest = product - piece_h.astype(F32)
    piece_m = rest.astype(BF16)
    piece_l = (rest - piece_m.astype(F32)).astype(BF16)
    tap_of = lax.broadcasted_iota(jnp.int32, (8, TAPS * 128), 1)
    row_of = lax.broadcasted_iota(jnp.int32, (8, TAPS * 128), 0)
    ones = jnp.where(lax.div(tap_of, 128) == row_of, 1.0, 0.0).astype(BF16)
    depth = dot_nt(ones, piece_h) + (dot_nt(ones, piece_m) + dot_nt(ones, piece_l))
    part[40] = jnp.concatenate([depth, jnp.zeros((8, 64), F32)], axis=1)

    for u, p in enumerate(owners):

        @pl.when(me != p)
        def _(u=u, p=p):
            device = (a_hi * low_chan + p // low_tm, b_hi * low_tm + p % low_tm)
            remote(part.at[PLANE_UNITS + u], plane_x.at[me], xssem.at[0], xrsem.at[0], device).start()

    for o in range(8):
        wide_taps = jnp.concatenate([hp[j, o + s] for j in range(3) for s in range(2)], axis=1)
        feat[o] = dot_nt(cwt[...], wide_taps).astype(BF16)

    plane_in[me] = part[me]
    several(plane_in, plane - 1, ssem.at[0], rsem.at[0]).wait_recv()
    total = plane_in[0]
    for d in range(1, plane):
        total = total + plane_in[d]
    mine[0] = total
    for device in in_tower:
        remote(mine.at[0], tower_in.at[level], ssem.at[1], rsem.at[1], device).start()

    def finish(m):
        unit = eye[0:128, 0:128]
        s = m % 4
        gd[s] = dot(ga[m], pwt2[...])
        total = gh_s[m, 32:544]
        for k in range(TAPS):
            at = 48 - 8 * k
            total = total + wrow[k : k + 1, :] * gd[s, at : at + 512]
        gsig[m] = dot_nt(unit, total.astype(BF16)).astype(BF16)

    for m in range(4):
        finish(m)

    @pl.when(own_x)
    def _():
        plane_x[me] = part[unit_x]
        several(plane_x, plane - 1, xssem.at[0], xrsem.at[0]).wait_recv()
        total = plane_x[0]
        for d in range(1, plane):
            total = total + plane_x[d]
        mine[1] = total
        for device in in_tower:
            remote(mine.at[1], tower_x.at[level], xssem.at[1], xrsem.at[1], device).start()

    tower_in[level] = mine[0]
    several(tower_in, tower - 1, ssem.at[1], rsem.at[1]).wait_recv()
    total = tower_in[0]
    for q in range(1, tower):
        total = total + tower_in[q]
    done[me] = total
    for _, device in in_plane:
        remote(done.at[me], done.at[me], ssem.at[2], rsem.at[2], device).start()

    for m in range(4, 8):
        finish(m)

    @pl.when(own_x)
    def _():
        tower_x[level] = mine[1]
        several(tower_x, tower - 1, xssem.at[1], xrsem.at[1]).wait_recv()
        total = tower_x[0]
        for q in range(1, tower):
            total = total + tower_x[q]
        done[unit_x] = total
        for _, device in in_plane:
            remote(done.at[unit_x], done.at[unit_x], xssem.at[2], xrsem.at[2], device).start()

    def tile(n):
        return done[n * 8 : n * 8 + 8].reshape(64, 128)

    def conv_tile(n):
        zero = jnp.zeros((64, 128), F32)
        return jnp.transpose(jnp.concatenate([tile(n), zero], axis=0))

    several(plane_in, plane - 1, ssem.at[2], rsem.at[2]).wait_recv()
    for n in range(4):
        turned = conv_tile(n)
        for half in range(2):
            i, j = (half + 1, n) if n < 3 else (0, half)
            conv_out[i, j] = turned[half * 64 : half * 64 + 64, 0:64]

    @pl.when(own_x)
    def _():
        several(plane_in, EXTRA_UNITS - 1, xssem.at[2], xrsem.at[2]).wait_recv()

    @pl.when(jnp.logical_not(own_x))
    def _():
        several(plane_in, EXTRA_UNITS, xssem.at[2], xrsem.at[2]).wait_recv()

    conv_out[0, 2] = conv_tile(4)[64:128, 0:64]
    point_out[...] = tile(4)[:, 0:64]
    depth_out[...] = done[40][0:TAPS, 0:64]

    for n in range(8):

        @pl.when(around[n][1])
        def _(n=n):
            copies[n].wait_send()

    several(plane_in, plane - 1, ssem.at[0], rsem.at[0]).wait_send()
    several(tower_in, tower - 1, ssem.at[1], rsem.at[1]).wait_send()
    several(plane_in, plane - 1, ssem.at[2], rsem.at[2]).wait_send()

    @pl.when(own_x)
    def _():
        several(plane_in, EXTRA_UNITS - 1, xssem.at[0], xrsem.at[0]).wait_send()
        several(tower_in, tower - 1, xssem.at[1], xrsem.at[1]).wait_send()
        several(plane_in, plane - 1, xssem.at[2], xrsem.at[2]).wait_send()

    @pl.when(jnp.logical_not(own_x))
    def _():
        several(plane_in, EXTRA_UNITS, xssem.at[0], xrsem.at[0]).wait_send()


def emit_kernel(*refs):
    srcs, dsts, sem = refs[:5], refs[5:10], refs[10]
    copies = [pltpu.make_async_copy(src, dst, sem.at[n]) for n, (src, dst) in enumerate(zip(srcs, dsts))]
    for copy in copies:
        copy.start()
    for copy in copies:
        copy.wait()


def put(ref, unit, tile):
    ref[unit : unit + 8] = tile.reshape(8, 8, 128)


def solution(mesh):
    n_chan, n_tm = mesh.shape["chan"], mesh.shape["tm"]
    low_chan, low_tm = 8, 4
    plane = low_chan * low_tm
    tower = n_chan * n_tm // plane
    whole = pl.BlockSpec(memory_space=pltpu.VMEM)
    sems = pltpu.SemaphoreType.DMA((3,))
    hbm = pl.BlockSpec(memory_space=pltpu.MemorySpace.HBM)
    vm = pltpu.VMEM

    def local(signal, depth_weight, point_weight, conv_weight, grad_out):
        outs = pl.pallas_call(
            functools.partial(kernel, low_chan, low_tm, n_chan, n_tm),
            out_shape=(shapes := [
                jax.ShapeDtypeStruct((8, 64, 256), BF16),
                jax.ShapeDtypeStruct((8, 128, 512), BF16),
                jax.ShapeDtypeStruct((TAPS, 64), F32),
                jax.ShapeDtypeStruct((64, 64), F32),
                jax.ShapeDtypeStruct((3, 3, 64, 64), F32),
            ]),
            in_specs=[hbm] * 5,
            out_specs=[whole] * 5,
            scratch_shapes=[
                vm((8, 128, 512), BF16),
                vm((8, 64, 256), BF16),
                vm((TAPS, 64), F32),
                vm((64, 64), BF16),
                vm((3, 3, 64, 64), BF16),
                pltpu.SemaphoreType.DMA((5,)),
                vm((9, 64, 128), BF16),
                vm((9, 64, 128), BF16),
                vm((9, 64, 128), BF16),
                vm((9, 64, 128), BF16),
                vm((64, 512), BF16),
                vm((EDGE_G, 128), BF16),
                vm((EDGE_G, 128), BF16),
                vm((9, 608, 128), F32),
                vm((9, 560, 128), F32),
                vm((9, 560, 128), F32),
                vm((9, 560, 128), F32),
                vm((3, 9, 256, 128), BF16),
                vm((576, 256), BF16),
                vm((BWD_UNROLL, 296, 128), F32),
                vm((8, 576, 128), F32),
                vm((8, 560, 128), BF16),
                vm((BWD_UNROLL, 560, 128), BF16),
                vm((4, 560, 128), F32),
                vm((128, 896), F32),
                vm((256, 256), BF16),
                vm((256, 256), BF16),
                vm((64, 768), BF16),
                vm((128, 128), BF16),
                vm((128, 128), BF16),
                vm((8, 128), F32),
                vm((PLANE_UNITS + EXTRA_UNITS, 8, 128), F32),
                vm((plane, 8, 128), F32),
                vm((plane, 8, 128), F32),
                vm((2, 8, 128), F32),
                vm((tower, 8, 128), F32),
                vm((tower, 8, 128), F32),
                vm((PLANE_UNITS + EXTRA_UNITS, 8, 128), F32),
                pltpu.SemaphoreType.DMA((8,)),
                pltpu.SemaphoreType.DMA((8,)),
                sems, sems, sems, sems,
            ],
            compiler_params=pltpu.CompilerParams(
                collective_id=0, has_side_effects=True, vmem_limit_bytes=48 * 1024 * 1024
            ),
            name="step",
        )(
            *(
                pltpu.with_memory_space_constraint(x, pltpu.MemorySpace.HBM)
                for x in (signal.reshape(8, 128, 512), grad_out, depth_weight.T, point_weight, conv_weight)
            )
        )
        feat, gsig, depth, point, conv = pl.pallas_call(
            emit_kernel,
            out_shape=shapes,
            in_specs=[pl.BlockSpec(memory_space=pl.ANY)] * 5,
            out_specs=[pl.BlockSpec(memory_space=pl.ANY)] * 5,
            scratch_shapes=[pltpu.SemaphoreType.DMA((5,))],
            compiler_params=pltpu.CompilerParams(vmem_limit_bytes=1024 * 1024),
            name="emit",
        )(*outs)
        return feat, gsig.reshape(16, 64, 512), depth.T, point, conv

    in_specs = (P("chan", None, "tm"), P(), P(), P(), P("chan", None, "tm"))
    out_specs = (P("chan", None, "tm"), P("chan", None, "tm"), P(), P(), P())
    return jax.shard_map(local, mesh=mesh, in_specs=in_specs, out_specs=out_specs, check_vma=False)
```

```python
import functools
import math

import jax
import jax.numpy as jnp
from jax import lax
from jax.experimental import pallas as pl
from jax.experimental.pallas import tpu as pltpu
from jax.sharding import PartitionSpec as P

F32, BF16 = jnp.float32, jnp.bfloat16
MESH = pl.DeviceIdType.MESH
TAPS = 7
RIM = 24
EDGE = 48
EDGE_G = 16
PLANE_UNITS = 32
EXTRA_UNITS = 9
BWD_UNROLL = 4


def dot(a, b):
    return lax.dot_general(a, b, (((1,), (0,)), ((), ())), preferred_element_type=F32)


def dot_nt(a, b):
    return lax.dot_general(a, b, (((1,), (1,)), ((), ())), preferred_element_type=F32)


def select_matrix(rows, cols, offset=0):
    r = lax.broadcasted_iota(jnp.int32, (rows, cols), 0)
    c = lax.broadcasted_iota(jnp.int32, (rows, cols), 1)
    return jnp.where(c == r + offset, 1.0, 0.0).astype(BF16)


def loop(lo, hi, body):
    def step(i, carry):
        body(i)
        return carry

    lax.fori_loop(lo, hi, step, 0)


C0 = math.sqrt(2.0 / math.pi)
C1 = 0.044715 * C0


def gelu_cdf(pre):
    return 0.5 + 0.5 * jnp.tanh(pre * (C0 + C1 * (pre * pre)))


def gelu_slope(pre, cdf):
    return cdf + (pre * cdf) * (1.0 - cdf) * (2.0 * C0 + (6.0 * C1) * (pre * pre))


def kernel(
    low_chan, low_tm, n_chan, n_tm,
    sig_hbm, go_hbm, dw_hbm, pw_hbm, cw_hbm,
    feat, gsig, depth_out, point_out, conv_out,
    sig, go, dw, pw, cw, insem,
    send_l, send_r, halo_l, halo_r, row, corner_l, corner_r,
    xt, pre_s, cdf_s, ht, hp, go_next, gt, gh_s, ga, gb, gd, acc_m, eye, wup, cwt, pw2, pwt2, wrow,
    part, plane_in, plane_x, mine, tower_in, tower_x, done,
    hssem, hrsem, ssem, rsem, xssem, xrsem,
):
    loads = [
        pltpu.make_async_copy(src, dst, insem.at[n])
        for n, (src, dst) in enumerate(
            ((sig_hbm, sig), (go_hbm, go), (dw_hbm, dw), (pw_hbm, pw), (cw_hbm, cw))
        )
    ]
    for load in loads:
        load.start()

    a, b = lax.axis_index("chan"), lax.axis_index("tm")
    plane = low_chan * low_tm
    hi_tm = n_tm // low_tm
    tower = (n_chan // low_chan) * hi_tm
    a_hi, b_hi = lax.div(a, low_chan), lax.div(b, low_tm)
    a_lo, b_lo = lax.rem(a, low_chan), lax.rem(b, low_tm)
    me = a_lo * low_tm + b_lo
    level = a_hi * hi_tm + b_hi
    before_a, after_a = a > 0, a < n_chan - 1
    before_b, after_b = b > 0, b < n_tm - 1
    both_of = jnp.logical_and

    rows_at = [lax.rem(a_lo + i, low_chan) for i in range(low_chan)]
    cols_at = [lax.rem(b_lo + j, low_tm) for j in range(low_tm)]
    in_plane = [
        (r * low_tm + c, (a_hi * low_chan + r, b_hi * low_tm + c))
        for i, r in enumerate(rows_at)
        for j, c in enumerate(cols_at)
        if i + j > 0
    ]
    hi_chan = n_chan // low_chan
    levels_a = [lax.rem(a_hi + i, hi_chan) * low_chan + a_lo for i in range(hi_chan)]
    levels_b = [lax.rem(b_hi + j, hi_tm) * low_tm + b_lo for j in range(hi_tm)]
    in_tower = [
        (ra, rb) for i, ra in enumerate(levels_a) for j, rb in enumerate(levels_b) if i + j > 0
    ]

    owners = [3 * u for u in range(EXTRA_UNITS)]
    own_x = both_of(lax.rem(me, 3) == 0, me < 3 * EXTRA_UNITS)
    unit_x = PLANE_UNITS + lax.rem(lax.div(me, 3), EXTRA_UNITS)

    around = [
        ((a, b - 1), before_b, after_b),
        ((a, b + 1), after_b, before_b),
        ((a + 1, b), after_a, before_a),
        ((a - 1, b), before_a, after_a),
        ((a + 1, b - 1), both_of(after_a, before_b), both_of(before_a, after_b)),
        ((a + 1, b + 1), both_of(after_a, after_b), both_of(before_a, before_b)),
        ((a - 1, b - 1), both_of(before_a, before_b), both_of(after_a, after_b)),
        ((a - 1, b + 1), both_of(before_a, after_b), both_of(after_a, before_b)),
    ]
    barrier = pltpu.get_barrier_semaphore()
    greeted = plane + tower - 2
    for device, there, _ in around:
        greeted = greeted + there.astype(jnp.int32)

        @pl.when(there)
        def _(device=device):
            pl.semaphore_signal(barrier, inc=1, device_id=device, device_id_type=MESH)

    for device in in_tower + [device for _, device in in_plane]:
        pl.semaphore_signal(barrier, inc=1, device_id=device, device_id_type=MESH)

    eye[...] = select_matrix(256, 256)
    for load in loads[2:]:
        load.wait()
    lane = lax.broadcasted_iota(jnp.int32, (64, 128), 1)
    sub = lax.broadcasted_iota(jnp.int32, (64, 128), 0)
    twice16 = jnp.where(lax.rem(lane, 64) == sub, 1.0, 0.0).astype(BF16)
    r128 = lax.broadcasted_iota(jnp.int32, (128, 128), 0)
    c128 = lax.broadcasted_iota(jnp.int32, (128, 128), 1)
    same = (r128 < 64) == (c128 < 64)
    wide = dot(pw[...], twice16)
    pw2[...] = jnp.where(same, jnp.concatenate([wide, wide], axis=0), 0.0).astype(BF16)
    eye64 = select_matrix(64, 64)
    turned = dot(dot_nt(eye64, pw[...]).astype(BF16), twice16)
    pwt2[...] = jnp.where(same, jnp.concatenate([turned, turned], axis=0), 0.0).astype(BF16)
    zero64 = jnp.zeros((64, 64), BF16)
    wup[128:256, 0:128] = jnp.zeros((128, 128), BF16)
    for j in range(3):
        first = dot_nt(eye64, jnp.concatenate([zero64, cw[0, j]], axis=0)).astype(BF16)
        rest = dot_nt(eye64, jnp.concatenate([cw[1, j], cw[2, j]], axis=0)).astype(BF16)
        cwt[:, j * 256 : j * 256 + 128] = first
        cwt[:, j * 256 + 128 : j * 256 + 256] = rest
        at = {1: (0, 0), 2: (0, 128), 0: (128, 128)}[j]
        wup[at[0] : at[0] + 64, at[1] : at[1] + 128] = rest
        wup[at[0] + 64 : at[0] + 128, at[1] : at[1] + 128] = first
    wrow[0:TAPS, 0:64] = dw[...]
    wrow[0:TAPS, 64:128] = dw[...]
    wrow[TAPS:, :] = jnp.zeros((1, 128), F32)

    loads[1].wait()
    loads[0].wait()

    pick_s, pick_g = select_matrix(EDGE, 128), select_matrix(EDGE_G, 128)
    pick_sr, pick_gr = select_matrix(EDGE, 128, 128 - EDGE), select_matrix(EDGE_G, 128, 128 - EDGE_G)
    zero16 = jnp.zeros((64, 128), BF16)
    for m in range(-1, 8):
        for pick, pick2, lanes, glanes, dst in (
            (pick_s, pick_g, slice(0, 128), slice(0, 128), send_l),
            (pick_sr, pick_gr, slice(384, 512), slice(128, 256), send_r),
        ):
            if m >= 0:
                dst[m + 1, 0:EDGE] = dot_nt(pick, sig[m, :, lanes]).astype(BF16)
            low = go[m, :, glanes] if m >= 0 else zero16
            high = go[m + 1, :, glanes] if m < 7 else zero16
            dst[m + 1, EDGE:] = dot_nt(pick2, jnp.concatenate([low, high], axis=0)).astype(BF16)

    pl.semaphore_wait(barrier, greeted)
    pieces = [
        (send_l.at[pl.ds(1, 8)], halo_r.at[pl.ds(1, 8)]),
        (send_r.at[pl.ds(1, 8)], halo_l.at[pl.ds(1, 8)]),
        (sig.at[7, pl.ds(64, 64)], row),
        (go.at[0], go_next),
        (send_l.at[8, pl.ds(0, EDGE)], halo_r.at[0, pl.ds(0, EDGE)]),
        (send_r.at[8, pl.ds(0, EDGE)], halo_l.at[0, pl.ds(0, EDGE)]),
        (send_l.at[0, pl.ds(EDGE, EDGE_G)], corner_r),
        (send_r.at[0, pl.ds(EDGE, EDGE_G)], corner_l),
    ]
    copies = [
        pltpu.make_async_remote_copy(
            src_ref=src, dst_ref=dst, send_sem=hssem.at[n], recv_sem=hrsem.at[n],
            device_id=around[n][0], device_id_type=MESH,
        )
        for n, (src, dst) in enumerate(pieces)
    ]
    for n in (2, 3, 0, 1, 4, 5, 6, 7):

        @pl.when(around[n][1])
        def _(n=n):
            copies[n].start()

    def arrive(n):
        dst = pieces[n][1]

        @pl.when(around[n][2])
        def _():
            copies[n].wait_recv()

        @pl.when(jnp.logical_not(around[n][2]))
        def _():
            dst[...] = jnp.zeros(dst.shape, BF16)

    def turn(n, x):
        unit = eye[...]
        xt[n, 48:304] = dot_nt(unit, x[:, 0:256])
        xt[n, 304:560] = dot_nt(unit, x[:, 256:512])


    def taps(n, lo, count):
        low = wrow[0:1, :] * xt[n, lo : lo + count]
        for k in range(1, TAPS):
            low = low + wrow[k : k + 1, :] * xt[n, lo + 8 * k : lo + 8 * k + count]
        return low.astype(BF16)

    def forward(n, lo, count, keep=True):
        pre = dot(taps(n, lo, count), pw2[...])
        cdf = gelu_cdf(pre)
        ht[n, lo : lo + count] = xt[n, lo + 24 : lo + 24 + count] + pre * cdf
        if keep:
            pre_s[n, lo : lo + count] = pre
            cdf_s[n, lo : lo + count] = cdf

    def widen(m, lo, count):
        here, later = gt[m, lo : lo + count], gt[m, lo + 1 : lo + count + 1]
        return jnp.concatenate([here.astype(BF16), later.astype(BF16)], axis=1)

    def interleave(m, at, up):
        count = up.shape[0]
        gh_s[m, pl.ds(at, count, stride=2), :] = up[:, 0:128]
        gh_s[m, pl.ds(at + 1, count, stride=2), :] = up[:, 128:256]

    def split(n, lo, count):
        for j in range(3):
            hp[j, n, lo : lo + count] = ht[n, pl.ds(23 + j + 2 * lo, count, stride=2), :].astype(BF16)

    for m in range(8):
        turn(m + 1, sig[m])
        forward(m + 1, 48, 464)
        if m < 7:
            gt[m, 16:272] = dot_nt(eye[...], jnp.concatenate([go[m], go[m + 1]], axis=0))
            interleave(m, 32, dot(widen(m, 16, 240), wup[...]))
        split(m + 1, 16, 224)

    arrive(0)
    arrive(1)
    for lo, src, at in ((0, halo_l, 0), (512, halo_r, 560)):
        for n in range(1, 9):
            xt[n, at : at + EDGE] = src[n, 0:EDGE].astype(F32)
        pre = dot(jnp.concatenate([taps(n, lo, 48) for n in range(1, 9)], axis=0), pw2[...])
        cdf = gelu_cdf(pre)
        value = pre * cdf
        for n in range(1, 9):
            own_rows = slice((n - 1) * 48, n * 48)
            ht[n, lo : lo + 48] = xt[n, lo + 24 : lo + 72] + value[own_rows]
            pre_s[n, lo : lo + 48] = pre[own_rows]
            cdf_s[n, lo : lo + 48] = cdf[own_rows]
    arrive(2)
    arrive(4)
    arrive(5)
    xt[0, 0:EDGE] = halo_l[0, 0:EDGE].astype(F32)
    turn(0, jnp.concatenate([jnp.zeros((64, 512), BF16), row[...]], axis=0))
    xt[0, 560:608] = halo_r[0, 0:EDGE].astype(F32)
    forward(0, 16, 528, False)

    @pl.when(b == 0)
    def _():
        for n in range(9):
            ht[n, 23:24] = jnp.zeros((1, 128), F32)
            pre_s[n, 0:24] = jnp.zeros((24, 128), F32)
            cdf_s[n, 0:24] = jnp.zeros((24, 128), F32)

    @pl.when(b == n_tm - 1)
    def _():
        for n in range(9):
            pre_s[n, 536:560] = jnp.zeros((24, 128), F32)
            cdf_s[n, 536:560] = jnp.zeros((24, 128), F32)

    split(0, 0, 256)
    for n in range(1, 9):
        split(n, 0, 16)
        split(n, 240, 16)

    grads = []
    for j in range(3):
        total = jnp.zeros((64, 256), F32)
        for o in range(8):
            total = total + dot(go[o], jnp.concatenate([hp[j, o], hp[j, o + 1]], axis=1))
        grads.append(total)
        put(part, 8 * j, total[:, 128:256])
    put(part, 24, jnp.where(lane < 64, pltpu.roll(grads[0][:, 0:128], 64, 1), grads[1][:, 0:128]))
    last = grads[2][:, 0:128]

    def remote(src, dst, s, r, device):
        return pltpu.make_async_remote_copy(
            src_ref=src, dst_ref=dst, send_sem=s, recv_sem=r, device_id=device, device_id_type=MESH
        )

    def several(ref, count, sem_s, sem_r):
        at = ref.at[pl.ds(0, count)]
        return remote(at, at, sem_s, sem_r, in_plane[0][1])

    for p, device in in_plane:
        remote(part.at[p], plane_in.at[me], ssem.at[0], rsem.at[0], device).start()

    arrive(3)
    arrive(6)
    arrive(7)
    for halo, corner in ((halo_l, corner_l), (halo_r, corner_r)):
        halo[8, EDGE:] = (halo[8, EDGE:].astype(F32) + corner[...].astype(F32)).astype(BF16)

    for m in range(8):
        gt[m, 0:16] = halo_l[m + 1, EDGE:].astype(F32)
        gt[m, 272:288] = halo_r[m + 1, EDGE:].astype(F32)
        gt[m, 288:296] = jnp.zeros((8, 128), F32)
    gt[7, 16:272] = dot_nt(eye[...], jnp.concatenate([go[7], go_next[...]], axis=0))
    rims = [widen(m, lo, count) for m in range(7) for lo, count in ((0, 16), (256, 32))]
    up = dot(jnp.concatenate(rims + [widen(7, 0, 288)], axis=0), wup[...])
    for m in range(7):
        interleave(m, 0, up[48 * m : 48 * m + 16])
        interleave(m, 512, up[48 * m + 16 : 48 * m + 48])
    interleave(7, 0, up[336:624])

    def backward(i):
        lhs, rhs = [], []
        for s in range(BWD_UNROLL):
            m = BWD_UNROLL * i + s
            mixed = gh_s[m, 8:568] * gelu_slope(pre_s[m + 1], cdf_s[m + 1])
            ga[m] = mixed.astype(BF16)
            gb[s, 0:552] = mixed[8:560].astype(BF16)
            shifted = []
            for k in range(TAPS):
                at = 48 - 8 * k
                shifted.append(ga[m, at : at + 512] if k % 2 == 0 else gb[s, at - 8 : at + 504])
            lhs.append(sig[m])
            rhs.append(jnp.concatenate(shifted, axis=1))
        acc_m[...] += dot(jnp.concatenate(lhs, axis=1), jnp.concatenate(rhs, axis=0))

    acc_m[...] = jnp.zeros_like(acc_m)
    dw_col = jnp.transpose(jnp.concatenate([wrow[...], jnp.zeros((120, 128), F32)], axis=0))
    loop(0, 8 // BWD_UNROLL, backward)

    point = jnp.zeros((64, 128), F32)
    pw_wide = jnp.where(lane < 64, dot(pw[...], twice16), 0.0)
    products = []
    for k in range(TAPS):
        tap = acc_m[0:64, k * 128 : k * 128 + 128] + pltpu.roll(
            acc_m[64:128, k * 128 : k * 128 + 128], 64, 1
        )
        point = point + dw_col[0:64, k : k + 1] * tap
        products.append(tap * pw_wide)
    put(part, 32, jnp.where(lane < 64, point, last))
    product = jnp.concatenate(products, axis=1)
    piece_h = product.astype(BF16)
    rest = product - piece_h.astype(F32)
    piece_m = rest.astype(BF16)
    piece_l = (rest - piece_m.astype(F32)).astype(BF16)
    tap_of = lax.broadcasted_iota(jnp.int32, (8, TAPS * 128), 1)
    row_of = lax.broadcasted_iota(jnp.int32, (8, TAPS * 128), 0)
    ones = jnp.where(lax.div(tap_of, 128) == row_of, 1.0, 0.0).astype(BF16)
    depth = dot_nt(ones, piece_h) + (dot_nt(ones, piece_m) + dot_nt(ones, piece_l))
    part[40] = jnp.concatenate([depth, jnp.zeros((8, 64), F32)], axis=1)

    for u, p in enumerate(owners):

        @pl.when(me != p)
        def _(u=u, p=p):
            device = (a_hi * low_chan + p // low_tm, b_hi * low_tm + p % low_tm)
            remote(part.at[PLANE_UNITS + u], plane_x.at[me], xssem.at[0], xrsem.at[0], device).start()

    plane_in[me] = part[me]
    several(plane_in, plane - 1, ssem.at[0], rsem.at[0]).wait_recv()
    total = plane_in[0]
    for d in range(1, plane):
        total = total + plane_in[d]
    mine[0] = total
    for device in in_tower:
        remote(mine.at[0], tower_in.at[level], ssem.at[1], rsem.at[1], device).start()

    for o in range(8):
        wide_taps = jnp.concatenate([hp[j, o + s] for j in range(3) for s in range(2)], axis=1)
        feat[o] = dot_nt(cwt[...], wide_taps).astype(BF16)

    def finish(m):
        unit = eye[0:128, 0:128]
        s = m % 4
        gd[s] = dot(ga[m], pwt2[...])
        total = gh_s[m, 32:544]
        for k in range(TAPS):
            at = 48 - 8 * k
            total = total + wrow[k : k + 1, :] * gd[s, at : at + 512]
        gsig[m] = dot_nt(unit, total.astype(BF16)).astype(BF16)

    for m in range(4):
        finish(m)

    @pl.when(own_x)
    def _():
        plane_x[me] = part[unit_x]
        several(plane_x, plane - 1, xssem.at[0], xrsem.at[0]).wait_recv()
        total = plane_x[0]
        for d in range(1, plane):
            total = total + plane_x[d]
        mine[1] = total
        for device in in_tower:
            remote(mine.at[1], tower_x.at[level], xssem.at[1], xrsem.at[1], device).start()

    tower_in[level] = mine[0]
    several(tower_in, tower - 1, ssem.at[1], rsem.at[1]).wait_recv()
    total = tower_in[0]
    for q in range(1, tower):
        total = total + tower_in[q]
    done[me] = total
    for _, device in in_plane:
        remote(done.at[me], done.at[me], ssem.at[2], rsem.at[2], device).start()

    for m in range(4, 8):
        finish(m)

    @pl.when(own_x)
    def _():
        tower_x[level] = mine[1]
        several(tower_x, tower - 1, xssem.at[1], xrsem.at[1]).wait_recv()
        total = tower_x[0]
        for q in range(1, tower):
            total = total + tower_x[q]
        done[unit_x] = total
        for _, device in in_plane:
            remote(done.at[unit_x], done.at[unit_x], xssem.at[2], xrsem.at[2], device).start()

    def tile(n):
        return done[n * 8 : n * 8 + 8].reshape(64, 128)

    def conv_tile(n):
        zero = jnp.zeros((64, 128), F32)
        return jnp.transpose(jnp.concatenate([tile(n), zero], axis=0))

    several(plane_in, plane - 1, ssem.at[2], rsem.at[2]).wait_recv()
    for n in range(4):
        turned = conv_tile(n)
        for half in range(2):
            i, j = (half + 1, n) if n < 3 else (0, half)
            conv_out[i, j] = turned[half * 64 : half * 64 + 64, 0:64]

    @pl.when(own_x)
    def _():
        several(plane_in, EXTRA_UNITS - 1, xssem.at[2], xrsem.at[2]).wait_recv()

    @pl.when(jnp.logical_not(own_x))
    def _():
        several(plane_in, EXTRA_UNITS, xssem.at[2], xrsem.at[2]).wait_recv()

    conv_out[0, 2] = conv_tile(4)[64:128, 0:64]
    point_out[...] = tile(4)[:, 0:64]
    depth_out[...] = done[40][0:TAPS, 0:64]

    for n in range(8):

        @pl.when(around[n][1])
        def _(n=n):
            copies[n].wait_send()

    several(plane_in, plane - 1, ssem.at[0], rsem.at[0]).wait_send()
    several(tower_in, tower - 1, ssem.at[1], rsem.at[1]).wait_send()
    several(plane_in, plane - 1, ssem.at[2], rsem.at[2]).wait_send()

    @pl.when(own_x)
    def _():
        several(plane_in, EXTRA_UNITS - 1, xssem.at[0], xrsem.at[0]).wait_send()
        several(tower_in, tower - 1, xssem.at[1], xrsem.at[1]).wait_send()
        several(plane_in, plane - 1, xssem.at[2], xrsem.at[2]).wait_send()

    @pl.when(jnp.logical_not(own_x))
    def _():
        several(plane_in, EXTRA_UNITS, xssem.at[0], xrsem.at[0]).wait_send()


def emit_kernel(*refs):
    srcs, dsts, sem = refs[:5], refs[5:10], refs[10]
    copies = [pltpu.make_async_copy(src, dst, sem.at[n]) for n, (src, dst) in enumerate(zip(srcs, dsts))]
    for copy in copies:
        copy.start()
    for copy in copies:
        copy.wait()


def put(ref, unit, tile):
    ref[unit : unit + 8] = tile.reshape(8, 8, 128)


def solution(mesh):
    n_chan, n_tm = mesh.shape["chan"], mesh.shape["tm"]
    low_chan, low_tm = 8, 4
    plane = low_chan * low_tm
    tower = n_chan * n_tm // plane
    whole = pl.BlockSpec(memory_space=pltpu.VMEM)
    sems = pltpu.SemaphoreType.DMA((3,))
    hbm = pl.BlockSpec(memory_space=pltpu.MemorySpace.HBM)
    vm = pltpu.VMEM

    def local(signal, depth_weight, point_weight, conv_weight, grad_out):
        outs = pl.pallas_call(
            functools.partial(kernel, low_chan, low_tm, n_chan, n_tm),
            out_shape=(shapes := [
                jax.ShapeDtypeStruct((8, 64, 256), BF16),
                jax.ShapeDtypeStruct((8, 128, 512), BF16),
                jax.ShapeDtypeStruct((TAPS, 64), F32),
                jax.ShapeDtypeStruct((64, 64), F32),
                jax.ShapeDtypeStruct((3, 3, 64, 64), F32),
            ]),
            in_specs=[hbm] * 5,
            out_specs=[whole] * 5,
            scratch_shapes=[
                vm((8, 128, 512), BF16),
                vm((8, 64, 256), BF16),
                vm((TAPS, 64), F32),
                vm((64, 64), BF16),
                vm((3, 3, 64, 64), BF16),
                pltpu.SemaphoreType.DMA((5,)),
                vm((9, 64, 128), BF16),
                vm((9, 64, 128), BF16),
                vm((9, 64, 128), BF16),
                vm((9, 64, 128), BF16),
                vm((64, 512), BF16),
                vm((EDGE_G, 128), BF16),
                vm((EDGE_G, 128), BF16),
                vm((9, 608, 128), F32),
                vm((9, 560, 128), F32),
                vm((9, 560, 128), F32),
                vm((9, 560, 128), F32),
                vm((3, 9, 256, 128), BF16),
                vm((64, 256), BF16),
                vm((8, 296, 128), F32),
                vm((8, 576, 128), F32),
                vm((8, 560, 128), BF16),
                vm((BWD_UNROLL, 560, 128), BF16),
                vm((4, 560, 128), F32),
                vm((128, 896), F32),
                vm((256, 256), BF16),
                vm((256, 256), BF16),
                vm((64, 768), BF16),
                vm((128, 128), BF16),
                vm((128, 128), BF16),
                vm((8, 128), F32),
                vm((PLANE_UNITS + EXTRA_UNITS, 8, 128), F32),
                vm((plane, 8, 128), F32),
                vm((plane, 8, 128), F32),
                vm((2, 8, 128), F32),
                vm((tower, 8, 128), F32),
                vm((tower, 8, 128), F32),
                vm((PLANE_UNITS + EXTRA_UNITS, 8, 128), F32),
                pltpu.SemaphoreType.DMA((8,)),
                pltpu.SemaphoreType.DMA((8,)),
                sems, sems, sems, sems,
            ],
            compiler_params=pltpu.CompilerParams(
                collective_id=0, has_side_effects=True, vmem_limit_bytes=48 * 1024 * 1024
            ),
            name="step",
        )(
            *(
                pltpu.with_memory_space_constraint(x, pltpu.MemorySpace.HBM)
                for x in (signal.reshape(8, 128, 512), grad_out, depth_weight.T, point_weight, conv_weight)
            )
        )
        feat, gsig, depth, point, conv = pl.pallas_call(
            emit_kernel,
            out_shape=shapes,
            in_specs=[pl.BlockSpec(memory_space=pl.ANY)] * 5,
            out_specs=[pl.BlockSpec(memory_space=pl.ANY)] * 5,
            scratch_shapes=[pltpu.SemaphoreType.DMA((5,))],
            compiler_params=pltpu.CompilerParams(vmem_limit_bytes=1024 * 1024),
            name="emit",
        )(*outs)
        return feat, gsig.reshape(16, 64, 512), depth.T, point, conv

    in_specs = (P("chan", None, "tm"), P(), P(), P(), P("chan", None, "tm"))
    out_specs = (P("chan", None, "tm"), P("chan", None, "tm"), P(), P(), P())
    return jax.shard_map(local, mesh=mesh, in_specs=in_specs, out_specs=out_specs, check_vma=False)
```
